512 devices in a mesh: warp: 32 (over z_hi, x, core), weft: 16 (over y, z_lo).
Axes of the slice: x: 4, y: 4, z: 16 (z_hi: 4, z_lo: 4; z = z_hi * 4 + z_lo), core: 2. Of those that a mesh axis runs over, the one named last changes fastest.
Arguments:
- fabric_state: float32 [1, 8, 256, 2048], P(None, None, 'warp', 'weft'), may hold values from -3 to 3
- final_adjoint: float32 [1, 8, 256, 2048], P(None, None, 'warp', 'weft'), may hold values from -6 to 6
- stiffness: float32 [2, 256, 2048], P(None, 'warp', 'weft'), may hold values from 0.5 to 2
- pinned: int32 [1, 256, 2048], P(None, 'warp', 'weft'), may hold values 0 or 1
- weave_codes: int32 [256, 2048], P('warp', 'weft'), may hold values from 0 to 3
- first_weight: bfloat16 [12, 256], replicated, may hold values from -1.75 to 1.75
- second_weight: bfloat16 [256, 256], replicated, may hold values from -0.375 to 0.375
- third_weight: bfloat16 [256, 2], replicated, may hold values from -0.375 to 0.375
Outputs:
- final_state: float32 [1, 8, 256, 2048], P(None, None, 'warp', 'weft')
- state_adjoint: float32 [1, 8, 256, 2048], P(None, None, 'warp', 'weft')
- first_grad: float32 [12, 256], replicated
- second_grad: float32 [256, 256], replicated
- third_grad: float32 [256, 2], replicated
The draws below stay inside these ranges and needn't reach their ends.
Inputs may be any that keep to these rules, and one draw needn't show every extreme that they name: `pinned`: 1 marks a crossing held fixed in that drape condition. `weave_codes`: bit 0 tells whether the warp passes over, bit 1 the weave's second pattern bit.
All inputs are finite; a program needn't handle non-finite values. No bound on the sum of `pinned` on one device may be relied on, other than what follows from the above.
Results may differ from the reference program's by a relative error of at most 0.0049.
Values sent between devices are 32-bit elements; how exact they have to be, the bound alone decides.
No kernel may reach another device: no remote copies, remote signals or barrier semaphores. Data moves between devices by JAX's collectives and lax.ppermute only.
A program may use at most 64 MiB of HBM per device.

```python
import math
import jax
import jax.numpy as jnp
from jax import lax

COND = 1
SUBSTEPS = 3
F_IN = 12
HID = 256
NX = 256
NY = 2048


def with_ends(array, rng, least, largest):
    spot = [jax.random.randint(jax.random.fold_in(rng, axis), (), 0, length) for axis, length in enumerate(array.shape)]
    longest = array.shape.index(max(array.shape))
    neighbour = spot[:longest] + [(spot[longest] + 1) % array.shape[longest]] + spot[longest + 1:]
    return array.at[tuple(spot)].set(least).at[tuple(neighbour)].set(largest)


def shard_levels(rng, extent, pieces, low, top_value):
    def one(dim, parts):
        heights = jax.random.uniform(jax.random.fold_in(jax.random.fold_in(rng, 6), dim), (parts,), jnp.float32, low / len(pieces), top_value / len(pieces))
        return jnp.repeat(jnp.exp(heights), extent[dim] // parts).reshape((-1,) + (1,) * (len(extent) - dim - 1))

    level = one(*pieces[0])
    for cut in pieces[1:]:
        level = level * one(*cut)
    return level


def scatter_about(rng, extent, scale, limit, cuts=(), dtype=jnp.bfloat16):
    entries = jax.random.normal(rng, extent, jnp.float32) * scale
    if len(cuts) > 0:
        entries = shard_levels(rng, extent, cuts, -0.22, 0.18) * entries
    return jnp.clip(entries, min=-limit, max=limit).astype(dtype)


def setup_inputs(seed: int = 0) -> dict:
    key_list = jax.random.split(jax.random.key(seed), 9)
    return {
        "fabric_state": scatter_about(key_list[0], (COND, 8, NX, NY), 0.5, 3.0, ((2, 32), (3, 16)), jnp.float32),
        "final_adjoint": scatter_about(key_list[1], (COND, 8, NX, NY), 1.0, 6.0, ((2, 32), (3, 16)), jnp.float32),
        "stiffness": jnp.clip(jnp.exp(math.log(2.0) - 1.3862944 * jax.random.uniform(key_list[2], (2, NX, NY), jnp.float32) ** shard_levels(key_list[2], (2, NX, NY), ((1, 32), (2, 16)), -0.2, 0.2)), 0.5, 2.0),
        "pinned": with_ends((jax.random.randint(key_list[3], (COND, NX, NY), 0, 8) < 1).astype(jnp.int32), jax.random.fold_in(key_list[3], 1), 0, 1),
        "weave_codes": with_ends(jax.random.randint(key_list[4], (NX, NY), 0, 4), jax.random.fold_in(key_list[4], 1), 0, 3).astype(jnp.int32),
        "first_weight": scatter_about(key_list[5], (F_IN, HID), F_IN ** -0.5, 1.75),
        "second_weight": scatter_about(key_list[6], (HID, HID), HID ** -0.5, 0.375),
        "third_weight": scatter_about(key_list[7], (HID, 2), HID ** -0.5, 0.375),
    }


time_step = 0.25
damping = 0.9
bending = 0.25
coupling = 0.5
sliding = 0.5
gravity = 0.3


def center(padded):
    return padded[..., 2:-2, 2:-2]


def laplace_rows(padded):
    return padded[..., 3:-1, 2:-2] + padded[..., 1:-3, 2:-2] - 2.0 * padded[..., 2:-2, 2:-2]


def laplace_columns(padded):
    return padded[..., 2:-2, 3:-1] + padded[..., 2:-2, 1:-3] - 2.0 * padded[..., 2:-2, 2:-2]


def slope_rows(padded):
    return 0.5 * (padded[..., 3:-1, 2:-2] - padded[..., 1:-3, 2:-2])


def slope_columns(padded):
    return 0.5 * (padded[..., 2:-2, 3:-1] - padded[..., 2:-2, 1:-3])


def bend_rows(padded):
    return (padded[..., 4:, 2:-2] - 4.0 * padded[..., 3:-1, 2:-2] + 6.0 * padded[..., 2:-2, 2:-2]
            - 4.0 * padded[..., 1:-3, 2:-2] + padded[..., :-4, 2:-2])


def bend_columns(padded):
    return (padded[..., 2:-2, 4:] - 4.0 * padded[..., 2:-2, 3:-1] + 6.0 * padded[..., 2:-2, 2:-2]
            - 4.0 * padded[..., 2:-2, 1:-3] + padded[..., 2:-2, :-4])


def features(padded, weave_codes):
    inner = center(padded)
    conditions = padded.shape[0]
    first_sign = (2 * (weave_codes % 2) - 1).astype(jnp.float32)
    second_sign = (2 * (weave_codes // 2) - 1).astype(jnp.float32)
    shape = (conditions,) + first_sign.shape
    fields = [inner[:, 6], inner[:, 7], inner[:, 3], inner[:, 4], inner[:, 5],
              laplace_rows(padded[:, 6]), laplace_columns(padded[:, 7]),
              slope_rows(padded[:, 0]), slope_columns(padded[:, 1]), inner[:, 2],
              jnp.broadcast_to(first_sign, shape), jnp.broadcast_to(second_sign, shape)]
    return jnp.stack(fields, axis=1)


def advance(padded, stiffness, free, friction):
    inner = center(padded)
    place = padded[:, 0:3]
    force = (stiffness[0] * laplace_rows(place) + stiffness[1] * laplace_columns(place)
             - bending * (bend_rows(place) + bend_columns(place)))
    normal = jnp.zeros_like(inner[:, 0]) - gravity
    extra = jnp.stack([coupling * slope_rows(padded[:, 6]), coupling * slope_columns(padded[:, 7]), normal], axis=1)
    force = force + extra
    velocity = free[:, None] * (damping * inner[:, 3:6] + time_step * force)
    place_new = inner[:, 0:3] + time_step * velocity
    slide_rate = sliding * jnp.stack([laplace_rows(padded[:, 6]), laplace_columns(padded[:, 7])], axis=1) - friction
    slide_new = inner[:, 6:8] + time_step * slide_rate
    return jnp.concatenate([place_new, velocity, slide_new], axis=1)


def flatten(field):
    return jnp.moveaxis(field, 1, 0).reshape(field.shape[1], -1)


def unflatten(flat, conditions, local_rows, local_columns):
    return jnp.moveaxis(flat.reshape(flat.shape[0], conditions, local_rows, local_columns), 0, 1)


def blocks_of(flat, width):
    return jnp.moveaxis(flat.reshape(flat.shape[0], -1, width), 1, 0)


def joined(blocked):
    return jnp.moveaxis(blocked, 0, 1).reshape(blocked.shape[1], -1)


def contract(left, right):
    return lax.dot_general(left, right, (((0,), (0,)), ((), ())), preferred_element_type=jnp.float32)


def outer_sum(left, right):
    return lax.dot_general(left, right, (((1,), (1,)), ((), ())), preferred_element_type=jnp.float32)


def hidden_layers(first_weight, second_weight, inputs):
    pre_first = contract(first_weight, inputs)
    act_first = jax.nn.silu(pre_first).astype(jnp.bfloat16)
    pre_second = contract(second_weight, act_first)
    act_second = jax.nn.silu(pre_second).astype(jnp.bfloat16)
    return pre_first, act_first, pre_second, act_second


def silu_slope(pre):
    sigmoid_value = jax.nn.sigmoid(pre)
    return sigmoid_value * (1.0 + pre * (1.0 - sigmoid_value))


def friction_block(weights, inputs):
    first_weight, second_weight, third_weight = weights
    layers = hidden_layers(first_weight, second_weight, inputs)
    return contract(third_weight, layers[3])


def friction_back(weights, inputs, upstream):
    first_weight, second_weight, third_weight = weights
    pre_first, act_first, pre_second, act_second = hidden_layers(first_weight, second_weight, inputs)
    upstream_low = upstream.astype(jnp.bfloat16)
    grad_third = outer_sum(act_second, upstream_low)
    back_second = (jnp.dot(third_weight, upstream_low, preferred_element_type=jnp.float32)
                   * silu_slope(pre_second)).astype(jnp.bfloat16)
    grad_second = outer_sum(act_first, back_second)
    back_first = (jnp.dot(second_weight, back_second, preferred_element_type=jnp.float32)
                  * silu_slope(pre_first)).astype(jnp.bfloat16)
    grad_first = outer_sum(inputs, back_first)
    feature_grad = jnp.dot(first_weight, back_first, preferred_element_type=jnp.float32)
    return feature_grad, (grad_first, grad_second, grad_third)


def friction_all(weights, inputs, width):
    def one_block(piece):
        return friction_block(weights, piece)
    return joined(lax.map(one_block, blocks_of(inputs, width)))


def friction_grads(weights, inputs, upstream, width):
    start = tuple(jnp.zeros(weight.shape, jnp.float32) for weight in weights)

    def one_block(carry, pair):
        feature_grad, grads = friction_back(weights, pair[0], pair[1])
        return (carry[0] + grads[0], carry[1] + grads[1], carry[2] + grads[2]), feature_grad

    totals, feature_blocks = lax.scan(one_block, start, (blocks_of(inputs, width), blocks_of(upstream, width)))
    return joined(feature_blocks), totals


def adjoint_local(adjoint, free, inputs, weights, width):
    conditions, _, local_rows, local_columns = adjoint.shape
    total_velocity = adjoint[:, 3:6] + time_step * adjoint[:, 0:3]
    force_adjoint = (free * time_step)[:, None] * total_velocity
    slide_adjoint = adjoint[:, 6:8]
    upstream = flatten(-time_step * slide_adjoint)
    feature_flat, grads = friction_grads(weights, inputs, upstream, width)
    feature_adjoint = unflatten(feature_flat, conditions, local_rows, local_columns)
    carried = jnp.concatenate([force_adjoint, time_step * sliding * slide_adjoint + feature_adjoint[:, 5:7],
                               feature_adjoint[:, 7:9]], axis=1)
    kept = (adjoint[:, 0:3], (free * damping)[:, None] * total_velocity + feature_adjoint[:, 2:5],
            slide_adjoint + feature_adjoint[:, 0:2], feature_adjoint[:, 9])
    return carried, kept, grads


def adjoint_finish(padded, stiff_pad, kept):
    place_adjoint, velocity_adjoint, slide_adjoint, normal_adjoint = kept
    force_pad = padded[:, 0:3]
    place = (place_adjoint + laplace_rows(stiff_pad[0] * force_pad) + laplace_columns(stiff_pad[1] * force_pad)
             - bending * (bend_rows(force_pad) + bend_columns(force_pad)))
    place = place + jnp.stack([-slope_rows(padded[:, 5]), -slope_columns(padded[:, 6]), normal_adjoint], axis=1)
    slide = slide_adjoint + jnp.stack([
        laplace_rows(padded[:, 3]) - coupling * slope_rows(padded[:, 0]),
        laplace_columns(padded[:, 4]) - coupling * slope_columns(padded[:, 1])], axis=1)
    return jnp.concatenate([place, velocity_adjoint, slide], axis=1)


def reference(fabric_state, final_adjoint, stiffness, pinned, weave_codes, first_weight, second_weight, third_weight):
    conditions, local_rows, local_columns = pinned.shape
    cells = conditions * local_rows * local_columns
    width = min(4096, cells)
    weights = (first_weight, second_weight, third_weight)
    free = 1.0 - pinned.astype(jnp.float32)
    saved = []
    current = fabric_state
    for substep in range(SUBSTEPS):
        padded = jnp.pad(current, ((0, 0), (0, 0), (2, 2), (2, 2)))
        inputs = flatten(features(padded, weave_codes)).astype(jnp.bfloat16)
        saved.append(inputs)
        friction = unflatten(friction_all(weights, inputs, width), conditions, local_rows, local_columns)
        current = advance(padded, stiffness, free, friction)
    final_state = current
    stiff_pad = jnp.pad(stiffness, ((0, 0), (2, 2), (2, 2)))
    adjoint = final_adjoint
    totals = tuple(jnp.zeros(weight.shape, jnp.float32) for weight in weights)
    for substep in reversed(range(SUBSTEPS)):
        carried, kept, grads = adjoint_local(adjoint, free, saved[substep], weights, width)
        totals = (totals[0] + grads[0], totals[1] + grads[1], totals[2] + grads[2])
        padded = jnp.pad(carried, ((0, 0), (0, 0), (2, 2), (2, 2)))
        adjoint = adjoint_finish(padded, stiff_pad, kept)
    scale = float(cells) ** -0.5
    return final_state, adjoint, totals[0] * scale, totals[1] * scale, totals[2] * scale
```

```python
import jax
import jax.numpy as jnp
from jax import lax
from jax.sharding import Mesh, PartitionSpec as P

SUBSTEPS = 3
WARP = ("zhi", "x", "core")
WEFT = ("y", "zlo")
PLANE = ("x", "core", "y")
COLUMN = ("zhi", "zlo")


time_step = 0.25
damping = 0.9
bending = 0.25
coupling = 0.5
sliding = 0.5
gravity = 0.3


def with_halo(block, sides, width):
    for axis, dim in sides:
        count = lax.axis_size(axis)
        forward = [(i, i + 1) for i in range(count - 1)]
        backward = [(target, source) for source, target in forward]
        low = lax.ppermute(
            lax.slice_in_dim(block, block.shape[dim] - width, None, axis=dim), axis, forward
        )
        high = lax.ppermute(lax.slice_in_dim(block, 0, width, axis=dim), axis, backward)
        block = jnp.concatenate([low, block, high], axis=dim)
    return block


def center(padded):
    return padded[..., 2:-2, 2:-2]


def laplace_rows(padded):
    return padded[..., 3:-1, 2:-2] + padded[..., 1:-3, 2:-2] - 2.0 * padded[..., 2:-2, 2:-2]


def laplace_columns(padded):
    return padded[..., 2:-2, 3:-1] + padded[..., 2:-2, 1:-3] - 2.0 * padded[..., 2:-2, 2:-2]


def slope_rows(padded):
    return 0.5 * (padded[..., 3:-1, 2:-2] - padded[..., 1:-3, 2:-2])


def slope_columns(padded):
    return 0.5 * (padded[..., 2:-2, 3:-1] - padded[..., 2:-2, 1:-3])


def bend_rows(padded):
    return (
        padded[..., 4:, 2:-2]
        - 4.0 * padded[..., 3:-1, 2:-2]
        + 6.0 * padded[..., 2:-2, 2:-2]
        - 4.0 * padded[..., 1:-3, 2:-2]
        + padded[..., :-4, 2:-2]
    )


def bend_columns(padded):
    return (
        padded[..., 2:-2, 4:]
        - 4.0 * padded[..., 2:-2, 3:-1]
        + 6.0 * padded[..., 2:-2, 2:-2]
        - 4.0 * padded[..., 2:-2, 1:-3]
        + padded[..., 2:-2, :-4]
    )


def features(padded, weave_codes):
    inner = center(padded)
    conditions = padded.shape[0]
    first_sign = (2 * (weave_codes % 2) - 1).astype(jnp.float32)
    second_sign = (2 * (weave_codes // 2) - 1).astype(jnp.float32)
    shape = (conditions,) + first_sign.shape
    fields = [
        inner[:, 6],
        inner[:, 7],
        inner[:, 3],
        inner[:, 4],
        inner[:, 5],
        laplace_rows(padded[:, 6]),
        laplace_columns(padded[:, 7]),
        slope_rows(padded[:, 0]),
        slope_columns(padded[:, 1]),
        inner[:, 2],
        jnp.broadcast_to(first_sign, shape),
        jnp.broadcast_to(second_sign, shape),
    ]
    return jnp.stack(fields, axis=1)


def advance(padded, stiffness, free, friction):
    inner = center(padded)
    place = padded[:, 0:3]
    force = (
        stiffness[0] * laplace_rows(place)
        + stiffness[1] * laplace_columns(place)
        - bending * (bend_rows(place) + bend_columns(place))
    )
    normal = jnp.zeros_like(inner[:, 0]) - gravity
    extra = jnp.stack(
        [coupling * slope_rows(padded[:, 6]), coupling * slope_columns(padded[:, 7]), normal],
        axis=1,
    )
    force = force + extra
    velocity = free[:, None] * (damping * inner[:, 3:6] + time_step * force)
    place_new = inner[:, 0:3] + time_step * velocity
    slide_rate = (
        sliding * jnp.stack([laplace_rows(padded[:, 6]), laplace_columns(padded[:, 7])], axis=1)
        - friction
    )
    slide_new = inner[:, 6:8] + time_step * slide_rate
    return jnp.concatenate([place_new, velocity, slide_new], axis=1)


def flatten(field):
    return jnp.moveaxis(field, 1, 0).reshape(field.shape[1], -1)


def unflatten(flat, conditions, local_rows, local_columns):
    return jnp.moveaxis(flat.reshape(flat.shape[0], conditions, local_rows, local_columns), 0, 1)


def blocks_of(flat, width):
    return jnp.moveaxis(flat.reshape(flat.shape[0], -1, width), 1, 0)


def joined(blocked):
    return jnp.moveaxis(blocked, 0, 1).reshape(blocked.shape[1], -1)


def contract(left, right):
    return lax.dot_general(
        left, right, (((0,), (0,)), ((), ())), preferred_element_type=jnp.float32
    )


def outer_sum(left, right):
    return lax.dot_general(
        left, right, (((1,), (1,)), ((), ())), preferred_element_type=jnp.float32
    )


def hidden_layers(first_weight, second_weight, inputs):
    pre_first = contract(first_weight, inputs)
    act_first = jax.nn.silu(pre_first).astype(jnp.bfloat16)
    pre_second = contract(second_weight, act_first)
    act_second = jax.nn.silu(pre_second).astype(jnp.bfloat16)
    return (pre_first, act_first, pre_second, act_second)


def silu_slope(pre):
    sigmoid_value = jax.nn.sigmoid(pre)
    return sigmoid_value * (1.0 + pre * (1.0 - sigmoid_value))


def friction_block(weights, inputs):
    first_weight, second_weight, third_weight = weights
    layers = hidden_layers(first_weight, second_weight, inputs)
    return contract(third_weight, layers[3])


def friction_back(weights, inputs, upstream):
    first_weight, second_weight, third_weight = weights
    pre_first, act_first, pre_second, act_second = hidden_layers(
        first_weight, second_weight, inputs
    )
    upstream_low = upstream.astype(jnp.bfloat16)
    grad_third = outer_sum(act_second, upstream_low)
    back_second = (
        jnp.dot(third_weight, upstream_low, preferred_element_type=jnp.float32)
        * silu_slope(pre_second)
    ).astype(jnp.bfloat16)
    grad_second = outer_sum(act_first, back_second)
    back_first = (
        jnp.dot(second_weight, back_second, preferred_element_type=jnp.float32)
        * silu_slope(pre_first)
    ).astype(jnp.bfloat16)
    grad_first = outer_sum(inputs, back_first)
    feature_grad = jnp.dot(first_weight, back_first, preferred_element_type=jnp.float32)
    return (feature_grad, (grad_first, grad_second, grad_third))


def friction_all(weights, inputs, width):

    def one_block(piece):
        return friction_block(weights, piece)

    return joined(lax.map(one_block, blocks_of(inputs, width)))


def friction_grads(weights, inputs, upstream, width):
    start = tuple((jnp.zeros(weight.shape, jnp.float32) for weight in weights))

    def one_block(carry, pair):
        feature_grad, grads = friction_back(weights, pair[0], pair[1])
        return ((carry[0] + grads[0], carry[1] + grads[1], carry[2] + grads[2]), feature_grad)

    totals, feature_blocks = lax.scan(
        one_block, start, (blocks_of(inputs, width), blocks_of(upstream, width))
    )
    return (joined(feature_blocks), totals)


def adjoint_local(adjoint, free, inputs, weights, width):
    conditions, _, local_rows, local_columns = adjoint.shape
    total_velocity = adjoint[:, 3:6] + time_step * adjoint[:, 0:3]
    force_adjoint = (free * time_step)[:, None] * total_velocity
    slide_adjoint = adjoint[:, 6:8]
    upstream = flatten(-time_step * slide_adjoint)
    feature_flat, grads = friction_grads(weights, inputs, upstream, width)
    feature_adjoint = unflatten(feature_flat, conditions, local_rows, local_columns)
    carried = jnp.concatenate(
        [
            force_adjoint,
            time_step * sliding * slide_adjoint + feature_adjoint[:, 5:7],
            feature_adjoint[:, 7:9],
        ],
        axis=1,
    )
    kept = (
        adjoint[:, 0:3],
        (free * damping)[:, None] * total_velocity + feature_adjoint[:, 2:5],
        slide_adjoint + feature_adjoint[:, 0:2],
        feature_adjoint[:, 9],
    )
    return (carried, kept, grads)


def adjoint_finish(padded, stiff_pad, kept):
    place_adjoint, velocity_adjoint, slide_adjoint, normal_adjoint = kept
    force_pad = padded[:, 0:3]
    place = (
        place_adjoint
        + laplace_rows(stiff_pad[0] * force_pad)
        + laplace_columns(stiff_pad[1] * force_pad)
        - bending * (bend_rows(force_pad) + bend_columns(force_pad))
    )
    place = place + jnp.stack(
        [-slope_rows(padded[:, 5]), -slope_columns(padded[:, 6]), normal_adjoint], axis=1
    )
    slide = slide_adjoint + jnp.stack(
        [
            laplace_rows(padded[:, 3]) - coupling * slope_rows(padded[:, 0]),
            laplace_columns(padded[:, 4]) - coupling * slope_columns(padded[:, 1]),
        ],
        axis=1,
    )
    return jnp.concatenate([place, velocity_adjoint, slide], axis=1)


def spread_field(current):
    return with_halo(current, ((WARP, 2), (WEFT, 3)), 2)


def spread_adjoint(carried):
    return with_halo(carried, ((WARP, 2), (WEFT, 3)), 2)


def sum_everywhere(totals):
    first, second, third = totals
    plane, column = lax.axis_size(PLANE), lax.axis_size(COLUMN)
    sizes = [second.size, first.size, third.size]
    flat = jnp.concatenate([second.reshape(-1), first.reshape(-1), third.reshape(-1)])
    rows = -(-flat.size // (plane * 128))
    rows = -(-rows // 8) * 8
    flat = jnp.pad(flat, (0, plane * rows * 128 - flat.size)).reshape(plane, rows, 128)
    part = jnp.sum(lax.all_to_all(flat, PLANE, 0, 0, tiled=True), axis=0)
    part = jnp.broadcast_to(part, (column,) + part.shape)
    part = jnp.sum(lax.all_to_all(part, COLUMN, 0, 0, tiled=True), axis=0)
    part = jnp.broadcast_to(part, (plane,) + part.shape)
    flat = lax.all_to_all(part, PLANE, 0, 0, tiled=True).reshape(-1)
    ends = [sizes[0], sizes[0] + sizes[1], sum(sizes)]
    return (
        flat[ends[0] : ends[1]].reshape(first.shape),
        flat[: ends[0]].reshape(second.shape),
        flat[ends[1] : ends[2]].reshape(third.shape),
    )


def shards(
    fabric_state,
    final_adjoint,
    stiffness,
    pinned,
    weave_codes,
    first_weight,
    second_weight,
    third_weight,
):
    conditions, local_rows, local_columns = pinned.shape
    cells = conditions * local_rows * local_columns
    width = min(512, cells)
    weights = (first_weight, second_weight, third_weight)
    free = 1.0 - pinned.astype(jnp.float32)
    saved = []
    current = fabric_state
    for substep in range(SUBSTEPS):
        padded = spread_field(current)
        inputs = flatten(features(padded, weave_codes)).astype(jnp.bfloat16)
        saved.append(inputs)
        friction = unflatten(
            friction_all(weights, inputs, width), conditions, local_rows, local_columns
        )
        current = advance(padded, stiffness, free, friction)
    stiff_pad = with_halo(stiffness, ((WARP, 1), (WEFT, 2)), 2)
    adjoint = final_adjoint
    collected = []
    for substep in reversed(range(SUBSTEPS)):
        carried, kept, grads = adjoint_local(adjoint, free, saved[substep], weights, width)
        collected.append(grads)
        adjoint = adjoint_finish(spread_adjoint(carried), stiff_pad, kept)
    local_totals = collected[0]
    for later in collected[1:]:
        local_totals = (
            local_totals[0] + later[0],
            local_totals[1] + later[1],
            local_totals[2] + later[2],
        )
    totals = sum_everywhere(local_totals)
    scale = float(cells * lax.axis_size(WARP) * lax.axis_size(WEFT)) ** (-0.5)
    return (current, adjoint, totals[0] * scale, totals[1] * scale, totals[2] * scale)


def factors(mesh):
    warp, weft = mesh.shape["warp"], mesh.shape["weft"]
    zlo = 4 if weft % 4 == 0 else 1
    x = 4 if warp % 8 == 0 else 1
    core = 2 if warp % 2 == 0 else 1
    return (warp // (x * core), x, core, weft // zlo, zlo)


def solution(mesh):
    fine = Mesh(mesh.devices.reshape(factors(mesh)), WARP + WEFT)
    placed = (
        P(None, None, WARP, WEFT),
        P(None, None, WARP, WEFT),
        P(None, WARP, WEFT),
        P(None, WARP, WEFT),
        P(WARP, WEFT),
        P(),
        P(),
        P(),
    )
    return jax.shard_map(
        shards,
        mesh=fine,
        in_specs=placed,
        out_specs=(P(None, None, WARP, WEFT), P(None, None, WARP, WEFT), P(), P(), P()),
        check_vma=False,
    )
```

```python
import functools

import jax
import jax.numpy as jnp
from jax import lax
from jax.experimental import pallas as pl
from jax.experimental.pallas import tpu as pltpu
from jax.sharding import Mesh, PartitionSpec as P

WARP = ("zhi", "x", "core")
WEFT = ("y", "zlo")
PLANE = ("x", "core", "y")
COLUMN = ("zhi", "zlo")

DT = 0.25
DAMP = 0.9
KB = 0.25
KC = 0.5
KS = 0.5
GRAV = 0.3

TILE_ROWS = 8
LANES = 128
REACH = 10
FIRST = REACH
ALL_ROWS = TILE_ROWS + 2 * REACH
HID = 256
CHUNK = 256
OWN = TILE_ROWS * LANES
F32 = jnp.float32
BF16 = jnp.bfloat16


def span(radius):
    return range(FIRST - radius, FIRST + TILE_ROWS + radius)


def distance(row):
    return max(FIRST - row, row - (FIRST + TILE_ROWS - 1), 0)


def ring(e):
    return [FIRST - e, FIRST + TILE_ROWS - 1 + e]


class Plan:
    def __init__(self, reach, back):
        self.reach, self.back = reach, back
        own = list(range(FIRST, FIRST + TILE_ROWS))
        order = own + [r for e in range(1, back + 1) for r in ring(e)]
        near = len(order)
        order = order + [None] + [r for e in range(back + 1, reach + 1) for r in ring(e)]
        self.tile = {r: t for t, r in enumerate(order) if r is not None}
        self.forward, self.backward = {}, {}
        at = {near: 0, len(order): 0}

        def put(table, row, tile, width):
            table[row] = (tile, at[tile], width)
            at[tile] += 2 * width

        for r in own:
            put(self.forward, r, near, reach)
            self.backward[r] = self.forward[r]
        for e in range(1, reach):
            width, need = reach - e, back - e
            for r in ring(e):
                if need > 0 and at[near] + 2 * width <= LANES and (e == 1 or reach == back):
                    put(self.forward, r, near, width)
                    self.backward[r] = self.forward[r]
                else:
                    put(self.forward, r, len(order), width)
                    if need > 0:
                        put(self.backward, r, near, need)
        self.packed = {near} | ({len(order)} if at[len(order)] else set())
        assert max(at.values()) <= LANES
        per = CHUNK // LANES
        tiles = len(order) + (1 if at[len(order)] else 0)
        self.chunks = -(-tiles // per)
        self.back_chunks = -(-(near + 1) // per)
        self.near = near
        self.lanes = self.chunks * CHUNK
        self.back_lanes = self.back_chunks * CHUNK
        self.spare = [t for t in range(tiles, self.chunks * per)]


PLANS = [Plan(7, 1), Plan(6, 3), Plan(5, 5)]


def dot(left, right):
    return lax.dot_general(left, right, (((1,), (0,)), ((), ())), preferred_element_type=F32)


def dot_rows(left, right):
    return lax.dot_general(left, right, (((1,), (1,)), ((), ())), preferred_element_type=F32)


def lane_index():
    return lax.broadcasted_iota(jnp.int32, (8, LANES), 1)


def field_index():
    return lax.broadcasted_iota(jnp.int32, (8, LANES), 0)


def pack_kernel(state_ref, adjoint_ref, stiff_ref, pinned_ref, weave_ref, own_ref, low_ref, high_ref):
    lane, field = lane_index(), field_index()
    low = [jnp.zeros((8, LANES), F32) for _ in range(3)]
    high = [jnp.zeros((8, LANES), F32) for _ in range(3)]
    for row in range(TILE_ROWS):
        k0 = stiff_ref[0, row : row + 1, :]
        k1 = stiff_ref[1, row : row + 1, :]
        free = 1.0 - pinned_ref[0, row : row + 1, :].astype(F32)
        code = weave_ref[row : row + 1, :]
        first_sign = (2 * jnp.bitwise_and(code, 1) - 1).astype(F32)
        second_sign = (2 * jnp.right_shift(code, 1) - 1).astype(F32)
        cell = jnp.where(field == 5, 1.0, 0.0)
        for place, value in enumerate((k0, k1, first_sign, second_sign, free)):
            cell = jnp.where(field == place, value, cell)
        at = REACH * row
        here = (lane >= at) & (lane < at + REACH)
        for part, value in enumerate((state_ref[0, :, row, :], adjoint_ref[0, :, row, :], cell)):
            own_ref[row, 8 * part : 8 * part + 8, :] = value
            low[part] = jnp.where(here, pltpu.roll(value, at, 1) if at else value, low[part])
            shift = (at + REACH) % LANES
            high[part] = jnp.where(here, pltpu.roll(value, shift, 1), high[part])
    for part in range(3):
        low_ref[8 * part : 8 * part + 8, :] = low[part]
        high_ref[8 * part : 8 * part + 8, :] = high[part]


def roll(value, shift, axis):
    shift = shift % value.shape[axis]
    return pltpu.roll(value, shift, axis) if shift else value


def main_kernel(
    own_ref,
    left_ref,
    right_ref,
    below_ref,
    above_ref,
    far_below_ref,
    far_above_ref,
    w1t_ref,
    w1_ref,
    w2t_ref,
    w2_ref,
    w3t_ref,
    w3_ref,
    final_ref,
    adjoint_ref,
    grads_ref,
    state_a,
    state_b,
    later,
    adjoint,
    k0_ref,
    k1_ref,
    mask_ref,
    sign_ref,
    force_ref,
    ahead_ref,
    behind_ref,
    sum_ref,
    x0,
    x1,
    x2,
    slope_first0,
    slope_first1,
    slope_first2,
    slope_second0,
    slope_second1,
    slope_second2,
    act_first,
    act_second,
    friction,
    upstream,
    feature_back,
    back_first,
    back_second,
    total_second,
    total_first,
    total_third,
):
    lane, field = lane_index(), field_index()
    zero = jnp.zeros((8, LANES), F32)
    xs = (x0, x1, x2)
    slopes_first = (slope_first0, slope_first1, slope_first2)
    slopes_second = (slope_second0, slope_second1, slope_second2)
    place = field < 3
    speed = (field >= 3) & (field < 6)
    slide = field >= 6

    def beside(low, high, row):
        at = REACH * row
        out = jnp.where(lane < REACH, roll(high, -at, 1), 0.0)
        return jnp.where(lane >= LANES - REACH, roll(low, LANES - REACH - at, 1), out)

    for row in range(ALL_ROWS):
        e = row - FIRST
        if e < -TILE_ROWS:
            block, inside, near = far_below_ref, e + TILE_ROWS + 2, e + 2 * TILE_ROWS
        elif e < 0:
            block, inside, near = below_ref, e + TILE_ROWS, e + TILE_ROWS
        elif e < TILE_ROWS:
            block, inside, near = own_ref, e, e
        elif e < 2 * TILE_ROWS:
            block, inside, near = above_ref, e - TILE_ROWS, e - TILE_ROWS
        else:
            block, inside, near = far_above_ref, e - 2 * TILE_ROWS, e - 2 * TILE_ROWS
        for part in range(3 if -TILE_ROWS <= e < 2 * TILE_ROWS else 1):
            at = slice(8 * part, 8 * part + 8)
            if block is own_ref:
                low, high = left_ref[at, :], right_ref[at, :]
            elif block is far_below_ref or block is far_above_ref:
                low, high = block[2, at, :], block[3, at, :]
            else:
                low, high = block[TILE_ROWS, at, :], block[TILE_ROWS + 1, at, :]
            pair = (block[inside, at, :], beside(low, high, near))
            for half in range(2):
                value = pair[half]
                if part == 0:
                    state_a[row, half] = value
                elif part == 1:
                    adjoint[row, half] = value
                else:
                    k0_ref[row, half] = jnp.broadcast_to(value[0:1], (8, LANES))
                    k1_ref[row, half] = jnp.broadcast_to(value[1:2], (8, LANES))
                    mask_ref[row, half] = jnp.where(
                        place, 1.0, jnp.where(speed, value[4:5], value[5:6])
                    )
                    sign_ref[row, half] = jnp.where((field == 2) | (field == 3), value, 0.0)

    def across(pair, step):
        turned = [roll(value, -step, 1) for value in pair]
        edge = lane >= LANES - step if step > 0 else lane < -step
        return jnp.where(edge, turned[1], turned[0]), jnp.where(edge, turned[0], turned[1])

    def both(ref, row):
        return ref[row, 0], ref[row, 1]

    def gather(total, value, entry):
        _, at, width = entry
        turned = roll(value, at + width, 1)
        return jnp.where((lane >= at) & (lane < at + 2 * width), turned, total)

    def scatter(value, entry):
        _, at, width = entry
        turned = roll(value, -(at + width), 1)
        return jnp.where((lane < width) | (lane >= LANES - width), turned, 0.0)

    def tile_lanes(tile):
        return slice(tile * LANES, (tile + 1) * LANES)

    gravity = jnp.where(field == 5, -GRAV, 0.0)
    keep = jnp.where(speed, DAMP, 1.0)

    def forward(k, state, target):
        plan = PLANS[k]
        x_ref = xs[k]
        moved = span((8, 6, 0)[k])
        packed = {tile: [zero, zero] for tile in plan.packed}
        for row in sorted(set(moved) | set(span(plan.reach))):
            here, up, down = both(state, row), both(state, row + 1), both(state, row - 1)
            right, left = across(here, 1), across(here, -1)
            update = row in moved
            if update:
                up2, down2 = both(state, row + 2), both(state, row - 2)
                right2, left2 = across(here, 2), across(here, -2)
            for half in range(2):
                s = here[half]
                twice = 2.0 * s
                lap_rows = up[half] + down[half] - twice
                lap_columns = right[half] + left[half] - twice
                slope_rows = 0.5 * (up[half] - down[half])
                slope_columns = 0.5 * (right[half] - left[half])
                if row in plan.tile:
                    mixed = jnp.where(field == 0, slope_rows, sign_ref[row, half])
                    mixed = jnp.where(field == 1, slope_columns, mixed)
                    mixed = jnp.where(field == 6, lap_rows, mixed)
                    mixed = jnp.where(field == 7, lap_columns, mixed)
                    if half == 0:
                        x_ref[:, tile_lanes(plan.tile[row])] = jnp.concatenate([s, mixed], axis=0).astype(BF16)
                    else:
                        for table in (plan.forward, plan.backward):
                            if row in table and (table is plan.forward or table[row] != plan.forward.get(row)):
                                entry = table[row]
                                old = packed[entry[0]]
                                packed[entry[0]] = [gather(old[0], s, entry), gather(old[1], mixed, entry)]
                if update and (half == 0 or k < 2):
                    bend = (up2[half] + down2[half] + right2[half] + left2[half]) - 4.0 * (
                        up[half] + down[half] + right[half] + left[half]
                    )
                    bend = bend + 12.0 * s
                    pull = k0_ref[row, half] * lap_rows + k1_ref[row, half] * lap_columns - KB * bend
                    turn = KC * jnp.where(field == 6, slope_rows, jnp.where(field == 7, slope_columns, 0.0))
                    force = roll(pull, 3, 0) + roll(turn, 5, 0) + gravity
                    rate = KS * jnp.where(field == 6, lap_rows, lap_columns)
                    change = jnp.where(speed, force, jnp.where(slide, rate, 0.0))
                    later[row, half] = keep * s + DT * change
        for tile, (top, bottom) in packed.items():
            x_ref[:, tile_lanes(tile)] = jnp.concatenate([top, bottom], axis=0).astype(BF16)
        for tile in plan.spare:
            x_ref[:, tile_lanes(tile)] = jnp.zeros((16, LANES), BF16)

        def network(c, own, saved):
            at = pl.ds(pl.multiple_of(c * CHUNK, CHUNK), CHUNK)
            z = dot(w1t_ref[...], x_ref[:, at])
            bent = jnp.tanh(z)
            part = z * bent
            act = (z + part).astype(BF16)
            if saved:
                slopes_first[k][:, at] = (1.0 + bent) * (1.0 + (z - part))
            if own:
                act_first[k, :, at] = act
            z = dot(w2t_ref[...], act)
            bent = jnp.tanh(z)
            part = z * bent
            act = (z + part).astype(BF16)
            if saved:
                slopes_second[k][:, at] = (1.0 + bent) * (1.0 + (z - part))
            if own:
                act_second[k, :, at] = act
            friction[:, at] = dot(w3t_ref[...], act)

        def loop(start, stop, own, saved):
            if stop > start:

                def body(c, carry):
                    network(c, own, saved)
                    return carry

                lax.fori_loop(start, stop, body, 0)

        loop(0, OWN // CHUNK, True, True)
        loop(OWN // CHUNK, plan.back_chunks, False, True)
        loop(plan.back_chunks, plan.chunks, False, False)
        for row in moved:
            for half in range(2 if k < 2 else 1):
                value = later[row, half]
                if half == 0 and row in plan.tile:
                    value = value - DT * friction[:, tile_lanes(plan.tile[row])]
                if half == 1 and row in plan.forward:
                    entry = plan.forward[row]
                    value = value - DT * scatter(friction[:, tile_lanes(entry[0])], entry)
                value = mask_ref[row, half] * value
                value = value + jnp.where(place, DT * roll(value, 5, 0), 0.0)
                if k < 2:
                    target[row, half] = value
                else:
                    final_ref[0, :, row - FIRST, :] = value

    forward(0, state_a, state_b)
    forward(1, state_b, state_a)
    forward(2, state_a, None)

    def backward(k):
        plan = PLANS[k]
        inner, middle, outer = plan.back - 1, plan.back, plan.back + 1
        packed = zero
        for row in span(middle):
            for half in range(2):
                value = jnp.where(slide, -DT * adjoint[row, half], 0.0)
                if half == 0:
                    upstream[:, tile_lanes(plan.tile[row])] = jnp.concatenate([value, zero], axis=0).astype(BF16)
                elif row in plan.backward:
                    packed = gather(packed, value, plan.backward[row])
        upstream[:, tile_lanes(plan.near)] = jnp.concatenate([packed, zero], axis=0).astype(BF16)
        for tile in range(plan.near + 1, plan.back_chunks * (CHUNK // LANES)):
            upstream[:, tile_lanes(tile)] = jnp.zeros((16, LANES), BF16)

        def network(c, own):
            at = pl.ds(pl.multiple_of(c * CHUNK, CHUNK), CHUNK)
            back = (dot(w3_ref[...], upstream[:, at]) * slopes_second[k][:, at]).astype(BF16)
            if own:
                back_second[:, at] = back
            back = (dot(w2_ref[...], back) * slopes_first[k][:, at]).astype(BF16)
            if own:
                back_first[:, at] = back
            feature_back[:, at] = dot(w1_ref[...], back)

        def loop(start, stop, own):
            def body(c, carry):
                network(c, own)
                return carry

            lax.fori_loop(start, stop, body, 0)

        loop(0, OWN // CHUNK, True)
        loop(OWN // CHUNK, plan.back_chunks, False)
        second = dot_rows(act_first[k], back_second[...])
        first = dot_rows(xs[k][:, 0:OWN], back_first[...])
        third = dot_rows(upstream[:, 0:OWN], act_second[k])
        if k == 2:
            total_second[...], total_first[...], total_third[...] = second, first, third
        else:
            total_second[...] += second
            total_first[...] += first
            total_third[...] += third

        for row in span(outer):
            for half in range(2):
                q = adjoint[row, half]
                total = mask_ref[row, half] * (q + DT * roll(q, 3, 0))
                force_ref[row, half] = jnp.where(place, DT * roll(total, 5, 0), 0.0)
                if distance(row) <= inner:
                    sum_ref[row, half] = jnp.where(speed, DAMP * total, q)
        for row in span(middle):
            force = both(force_ref, row)
            high, low = [], []
            for half in range(2):
                q, g = adjoint[row, half], force[half]
                if half == 0:
                    at = tile_lanes(plan.tile[row])
                    straight, mixed = feature_back[0:8, at], feature_back[8:16, at]
                elif row in plan.backward:
                    entry = plan.backward[row]
                    at = tile_lanes(entry[0])
                    straight, mixed = scatter(feature_back[0:8, at], entry), scatter(feature_back[8:16, at], entry)
                else:
                    straight, mixed = zero, zero
                carried = DT * KS * q + mixed
                by_rows = k0_ref[row, half] * g + jnp.where(field == 6, carried, 0.0)
                by_columns = k1_ref[row, half] * g + jnp.where(field == 7, carried, 0.0)
                tilt = 0.5 * jnp.where(slide, KC * roll(g, 6, 0), mixed)
                tilt_rows = jnp.where((field == 0) | (field == 6), tilt, 0.0)
                tilt_columns = jnp.where((field == 1) | (field == 7), tilt, 0.0)
                ahead_ref[row, half] = by_rows + 4.0 * KB * g - tilt_rows
                behind_ref[row, half] = by_rows + 4.0 * KB * g + tilt_rows
                high.append(by_columns + 4.0 * KB * g - tilt_columns)
                low.append(by_columns + 4.0 * KB * g + tilt_columns)
                if distance(row) <= inner:
                    center = -2.0 * (by_rows + by_columns) - 12.0 * KB * g
                    sum_ref[row, half] = sum_ref[row, half] + straight + center
            if distance(row) <= inner:
                right, left = across(high, 1), across(low, -1)
                right2, left2 = across(force, 2), across(force, -2)
                for half in range(2):
                    sideways = right[half] + left[half] - KB * (right2[half] + left2[half])
                    sum_ref[row, half] = sum_ref[row, half] + sideways
        for row in span(inner):
            for half in range(2 if k > 0 else 1):
                value = sum_ref[row, half] + ahead_ref[row + 1, half] + behind_ref[row - 1, half]
                value = value - KB * (force_ref[row + 2, half] + force_ref[row - 2, half])
                if k > 0:
                    adjoint[row, half] = jnp.where(slide, mask_ref[row, half] * value, value)
                else:
                    adjoint_ref[0, :, row - FIRST, :] = value

    backward(2)
    backward(1)
    backward(0)

    small = total_first[...]
    third = total_third[0:8, :]
    row_index = lax.broadcasted_iota(jnp.int32, (8, HID), 0)
    top = jnp.where(row_index < 2, pltpu.roll(third, 2, 0), small[0:8])
    bottom = small[8:16]
    for c in range(HID // 8):
        grads_ref[c, 0:8, :] = total_second[8 * c : 8 * c + 8, 0:LANES]
        grads_ref[c, 8:16, :] = total_second[8 * c : 8 * c + 8, LANES:]
        line = (top if c < 16 else bottom)[(c // 2) % 8 : (c // 2) % 8 + 1, (c % 2) * LANES : (c % 2 + 1) * LANES]
        grads_ref[c, 16:24, :] = jnp.broadcast_to(line, (8, LANES))


def run_main(*operands):
    rows = (ALL_ROWS, 2, 8, LANES)
    scratch = [pltpu.VMEM(rows, F32) for _ in range(12)]
    scratch += [pltpu.VMEM((16, plan.lanes), BF16) for plan in PLANS]
    scratch += [pltpu.VMEM((HID, plan.back_lanes), F32) for plan in PLANS] * 2
    scratch += [pltpu.VMEM((3, HID, OWN), BF16)] * 2
    scratch += [
        pltpu.VMEM((8, PLANS[0].lanes), F32),
        pltpu.VMEM((16, PLANS[2].back_lanes), BF16),
        pltpu.VMEM((16, PLANS[2].back_lanes), F32),
        pltpu.VMEM((HID, OWN), BF16),
        pltpu.VMEM((HID, OWN), BF16),
        pltpu.VMEM((HID, HID), F32),
        pltpu.VMEM((16, HID), F32),
        pltpu.VMEM((16, HID), F32),
    ]
    return pl.pallas_call(
        main_kernel,
        out_shape=(
            jax.ShapeDtypeStruct((1, 8, TILE_ROWS, LANES), F32),
            jax.ShapeDtypeStruct((1, 8, TILE_ROWS, LANES), F32),
            jax.ShapeDtypeStruct((HID // 8, 24, LANES), F32),
        ),
        scratch_shapes=scratch,
        name="substeps",
    )(*operands)


def run_pack(*operands):
    return pl.pallas_call(
        pack_kernel,
        out_shape=(
            jax.ShapeDtypeStruct((TILE_ROWS, 24, LANES), F32),
            jax.ShapeDtypeStruct((24, LANES), F32),
            jax.ShapeDtypeStruct((24, LANES), F32),
        ),
        name="pack_tile",
    )(*operands)


def shift(value, axis, step):
    count = lax.axis_size(axis)
    return lax.ppermute(value, axis, [(i, i + step) for i in range(count) if 0 <= i + step < count])


def sum_everywhere(part):
    plane, column = lax.axis_size(PLANE), lax.axis_size(COLUMN)
    part = jnp.sum(lax.all_to_all(part, PLANE, 0, 0, tiled=True), axis=0)
    part = jnp.broadcast_to(part, (column,) + part.shape)
    part = jnp.sum(lax.all_to_all(part, COLUMN, 0, 0, tiled=True), axis=0)
    part = jnp.broadcast_to(part, (plane,) + part.shape)
    return lax.all_to_all(part, PLANE, 0, 0, tiled=True)


def finish_kernel(scale, flat_ref, first_ref, second_ref, third_ref):
    for c in range(HID // 8):
        second_ref[8 * c : 8 * c + 8, 0:LANES] = flat_ref[c, 0:8, :] * scale
        second_ref[8 * c : 8 * c + 8, LANES:] = flat_ref[c, 8:16, :] * scale
    for half in range(2):
        at = slice(half * LANES, (half + 1) * LANES)
        for f, row in enumerate((6, 7, 3, 4, 5, 14, 15, 8, 9, 2, 10, 11)):
            first_ref[f : f + 1, at] = flat_ref[2 * row + half, 16:17, :] * scale
        for f in range(2):
            third_ref[f : f + 1, at] = flat_ref[2 * f + half, 16:17, :] * scale


def shards(state, adjoint, stiffness, pinned, weave, first_weight, second_weight, third_weight):
    own, low_edge, high_edge = run_pack(state, adjoint, stiffness, pinned, weave)
    left = shift(high_edge, WEFT, 1)
    right = shift(low_edge, WEFT, -1)
    wide = jnp.concatenate([own, left[None], right[None]], axis=0)
    sides = wide[TILE_ROWS:, 0:8]
    below = shift(wide, WARP, 1)
    above = shift(wide, WARP, -1)
    far_below = shift(jnp.concatenate([own[TILE_ROWS - 2 :, 0:8], sides], axis=0), WARP, 2)
    far_above = shift(jnp.concatenate([own[0:2, 0:8], sides], axis=0), WARP, -2)

    blank = jnp.zeros((2, HID), BF16)
    w = first_weight
    w1 = jnp.concatenate(
        [blank, w[9:10], w[2:5], w[0:2], w[7:9], w[10:12], blank, w[5:7]], axis=0
    )
    half = jnp.asarray(0.5, BF16)
    w1t = (half * w1).T
    w2 = half * second_weight
    w2t = w2.T
    w3t = jnp.pad(third_weight.T, ((6, 0), (0, 0)))
    w3 = jnp.pad(half * third_weight, ((0, 0), (6, 8)))
    final_state, state_adjoint, grads = run_main(
        own, left, right, below, above, far_below, far_above, w1t, w1, w2t, w2, w3t, w3
    )
    flat = sum_everywhere(grads)
    cells = OWN * lax.axis_size(WARP) * lax.axis_size(WEFT)
    first, second, third = pl.pallas_call(
        functools.partial(finish_kernel, float(cells) ** -0.5),
        out_shape=(
            jax.ShapeDtypeStruct((12, HID), F32),
            jax.ShapeDtypeStruct((HID, HID), F32),
            jax.ShapeDtypeStruct((2, HID), F32),
        ),
        name="unpack_grads",
    )(flat)
    return final_state, state_adjoint, first, second, third.T


def factors(mesh):
    warp, weft = mesh.shape["warp"], mesh.shape["weft"]
    zlo = 4 if weft % 4 == 0 else 1
    x = 4 if warp % 8 == 0 else 1
    core = 2 if warp % 2 == 0 else 1
    return (warp // (x * core), x, core, weft // zlo, zlo)


def solution(mesh):
    fine = Mesh(mesh.devices.reshape(factors(mesh)), WARP + WEFT)
    field = P(None, None, WARP, WEFT)
    placed = (field, field, P(None, WARP, WEFT), P(None, WARP, WEFT), P(WARP, WEFT), P(), P(), P())
    return jax.shard_map(
        shards,
        mesh=fine,
        in_specs=placed,
        out_specs=(field, field, P(), P(), P()),
        check_vma=False,
    )
```

```python
import functools

import jax
import jax.numpy as jnp
from jax import lax
from jax.experimental import pallas as pl
from jax.experimental.pallas import tpu as pltpu
from jax.sharding import Mesh, PartitionSpec as P

WARP = ("zhi", "x", "core")
WEFT = ("y", "zlo")
PLANE = ("x", "core", "y")
COLUMN = ("zhi", "zlo")

DT = 0.25
DAMP = 0.9
KB = 0.25
KC = 0.5
KS = 0.5
GRAV = 0.3

TILE_ROWS = 8
LANES = 128
REACH = 10
FIRST = REACH
ALL_ROWS = TILE_ROWS + 2 * REACH
HID = 256
OWN = TILE_ROWS * LANES
FEATURE_ROWS = (6, 7, 3, 4, 5, 14, 15, 8, 9, 2, 10, 11)
F32 = jnp.float32
BF16 = jnp.bfloat16


def span(radius):
    return range(FIRST - radius, FIRST + TILE_ROWS + radius)


def distance(row):
    return max(FIRST - row, row - (FIRST + TILE_ROWS - 1), 0)


def ring(e):
    return [FIRST - e, FIRST + TILE_ROWS - 1 + e]


class Plan:
    def __init__(self, reach, back):
        self.reach, self.back = reach, back
        own = list(range(FIRST, FIRST + TILE_ROWS))
        order = own + [r for e in range(1, back + 1) for r in ring(e)]
        near = len(order)
        order = order + [None] + [r for e in range(back + 1, reach + 1) for r in ring(e)]
        self.tile = {r: t for t, r in enumerate(order) if r is not None}
        self.forward, self.backward = {}, {}
        at = {near: 0, len(order): 0}

        def put(table, row, tile, width):
            table[row] = (tile, at[tile], width)
            at[tile] += 2 * width

        for r in own:
            put(self.forward, r, near, reach)
            self.backward[r] = self.forward[r]
        for e in range(1, reach):
            width, need = reach - e, back - e
            for r in ring(e):
                if need > 0 and at[near] + 2 * width <= LANES and (e == 1 or reach == back):
                    put(self.forward, r, near, width)
                    self.backward[r] = self.forward[r]
                else:
                    put(self.forward, r, len(order), width)
                    if need > 0:
                        put(self.backward, r, near, need)
        self.packed = {near} | ({len(order)} if at[len(order)] else set())
        assert max(at.values()) <= LANES
        self.near = near
        self.tiles = len(order) + (1 if at[len(order)] else 0)
        middle = {16: 16, 14: 15}.get(self.tiles - TILE_ROWS, self.tiles)
        self.saved = middle
        self.blocks = [(0, TILE_ROWS), (TILE_ROWS, middle)]
        if middle < self.tiles:
            self.blocks.append((middle, self.tiles))


PLANS = [Plan(7, 1), Plan(6, 3), Plan(5, 5)]


def dot(left, right):
    return lax.dot_general(left, right, (((1,), (0,)), ((), ())), preferred_element_type=F32)


def dot_columns(left, right):
    return lax.dot_general(left, right, (((0,), (0,)), ((), ())), preferred_element_type=F32)


def dot_rows(left, right):
    return lax.dot_general(left, right, (((1,), (1,)), ((), ())), preferred_element_type=F32)


def lane_index():
    return lax.broadcasted_iota(jnp.int32, (8, LANES), 1)


def field_index():
    return lax.broadcasted_iota(jnp.int32, (8, LANES), 0)


def pack_kernel(
    state_hbm, adjoint_hbm, stiff_hbm, pinned_hbm, weave_hbm, third_hbm,
    own_ref, low_ref, high_ref, last_ref,
    state_ref, adjoint_ref, stiff_ref, pinned_ref, weave_ref, third_ref, sems,
):
    sources = (state_hbm, adjoint_hbm, stiff_hbm, pinned_hbm, weave_hbm, third_hbm)
    targets = (state_ref, adjoint_ref, stiff_ref, pinned_ref, weave_ref, third_ref)
    copies = [pltpu.make_async_copy(a, b, sems.at[i]) for i, (a, b) in enumerate(zip(sources, targets))]
    for copy in copies:
        copy.start()
    for copy in copies:
        copy.wait()
    lane, field = lane_index(), field_index()
    last_ref[...] = jnp.zeros((1, 24, LANES), F32)
    third = third_ref[...].astype(F32)
    for f in range(2):
        last_ref[0, 2 * f : 2 * f + 1, :] = third[f : f + 1, 0:LANES]
        last_ref[0, 2 * f + 1 : 2 * f + 2, :] = third[f : f + 1, LANES:]
    low = [jnp.zeros((8, LANES), F32) for _ in range(3)]
    high = [jnp.zeros((8, LANES), F32) for _ in range(3)]
    for row in range(TILE_ROWS):
        k0 = stiff_ref[0, row : row + 1, :]
        k1 = stiff_ref[1, row : row + 1, :]
        free = 1.0 - pinned_ref[0, row : row + 1, :].astype(F32)
        code = weave_ref[row : row + 1, :]
        first_sign = (2 * jnp.bitwise_and(code, 1) - 1).astype(F32)
        second_sign = (2 * jnp.right_shift(code, 1) - 1).astype(F32)
        cell = jnp.where(field == 5, 1.0, 0.0)
        for place, value in enumerate((k0, k1, first_sign, second_sign, free)):
            cell = jnp.where(field == place, value, cell)
        at = REACH * row
        here = (lane >= at) & (lane < at + REACH)
        for part, value in enumerate((state_ref[0, :, row, :], adjoint_ref[0, :, row, :], cell)):
            own_ref[row, 8 * part : 8 * part + 8, :] = value
            low[part] = jnp.where(here, pltpu.roll(value, at, 1) if at else value, low[part])
            shift = (at + REACH) % LANES
            high[part] = jnp.where(here, pltpu.roll(value, shift, 1), high[part])
    for part in range(3):
        low_ref[8 * part : 8 * part + 8, :] = low[part]
        high_ref[8 * part : 8 * part + 8, :] = high[part]


def roll(value, shift, axis):
    shift = shift % value.shape[axis]
    return pltpu.roll(value, shift, axis) if shift else value


def main_kernel(
    own_ref,
    core_ref,
    partner_ref,
    cross_ref,
    far_ref,
    first_weight_ref,
    second_weight_ref,
    final_hbm,
    adjoint_hbm,
    grads_ref,
    final_ref,
    adjoint_ref,
    sems,
    state_a,
    state_b,
    later,
    adjoint,
    k0_ref,
    k1_ref,
    mask_ref,
    sign_ref,
    force_ref,
    ahead_ref,
    behind_ref,
    sum_ref,
    x0,
    x1,
    x2,
    slope_first0,
    slope_first1,
    slope_first2,
    slope_second0,
    slope_second1,
    slope_second2,
    act_first,
    act_second,
    friction,
    upstream,
    feature_back,
    total_second,
    total_first,
    total_third,
):
    lane, field = lane_index(), field_index()
    zero = jnp.zeros((8, LANES), F32)
    xs = (x0, x1, x2)
    slopes_first = (slope_first0, slope_first1, slope_first2)
    slopes_second = (slope_second0, slope_second1, slope_second2)
    f_row = lax.broadcasted_iota(jnp.int32, (16, 12), 0)
    f_column = lax.broadcasted_iota(jnp.int32, (16, 12), 1)
    chosen = jnp.zeros((16, 12), F32)
    for f, n in enumerate(FEATURE_ROWS):
        chosen = jnp.where((f_row == n) & (f_column == f), 1.0, chosen)
    w1_wide = dot(chosen.astype(BF16), first_weight_ref[...])
    w1, w1_half = w1_wide.astype(BF16), (0.5 * w1_wide).astype(BF16)
    w2 = (0.5 * second_weight_ref[...].astype(F32)).astype(BF16)
    f_row = lax.broadcasted_iota(jnp.int32, (16, 2), 0)
    f_column = lax.broadcasted_iota(jnp.int32, (16, 2), 1)
    third = [
        jnp.concatenate([own_ref[TILE_ROWS + 2, 2 * f + i : 2 * f + i + 1, :] for i in range(2)], axis=1)
        for f in range(2)
    ]
    third = jnp.concatenate(third, axis=0).astype(BF16)
    w3_wide = dot(jnp.where(f_row == f_column + 6, 1.0, 0.0).astype(BF16), third)
    w3t, w3 = w3_wide[0:8].astype(BF16), (0.5 * w3_wide).astype(BF16)
    place = field < 3
    speed = (field >= 3) & (field < 6)
    slide = field >= 6

    def beside(low, high, row):
        at = REACH * row
        out = jnp.where(lane < REACH, roll(high, -at, 1), 0.0)
        return jnp.where(lane >= LANES - REACH, roll(low, LANES - REACH - at, 1), out)

    first_core = core_ref[0] == 0

    def pick(lower, upper, at):
        return jnp.where(first_core, lower[at], upper[at])

    def received(e, part):
        at = slice(8 * part, 8 * part + 8)
        if e < -TILE_ROWS:
            i = e + TILE_ROWS + 2
            return [
                jnp.where(first_core, cross_ref[n, p, :], far_ref[m])
                for (n, p), m in zip(extra(i), (i, 2, 3))
            ]
        if e < 0:
            return [pick(cross_ref, partner_ref, (i, at)) for i in (e + TILE_ROWS, TILE_ROWS, TILE_ROWS + 1)]
        if e < TILE_ROWS:
            return [own_ref[i, at, :] for i in (e, TILE_ROWS, TILE_ROWS + 1)]
        if e < 2 * TILE_ROWS:
            return [pick(partner_ref, cross_ref, (i, at)) for i in (e - TILE_ROWS, TILE_ROWS, TILE_ROWS + 1)]
        i = e - 2 * TILE_ROWS
        return [
            jnp.where(first_core, far_ref[m], cross_ref[n, p, :])
            for (n, p), m in zip(extra(i), (i, 2, 3))
        ]

    def extra(i):
        n = TILE_ROWS + 2
        row = (n, slice(8 * i, 8 * i + 8))
        return row, (n, slice(16, 24)), (n + 1, slice(0, 8))

    for row in range(ALL_ROWS):
        e = row - FIRST
        near = e % TILE_ROWS
        for part in range(3 if -TILE_ROWS <= e < 2 * TILE_ROWS else 1):
            value, low, high = received(e, part)
            pair = (value, beside(low, high, near))
            for half in range(2):
                value = pair[half]
                if part == 0:
                    state_a[row, half] = value
                elif part == 1:
                    adjoint[row, half] = value
                else:
                    k0_ref[row, half] = jnp.broadcast_to(value[0:1], (8, LANES))
                    k1_ref[row, half] = jnp.broadcast_to(value[1:2], (8, LANES))
                    mask_ref[row, half] = jnp.where(
                        place, 1.0, jnp.where(speed, value[4:5], value[5:6])
                    )
                    sign_ref[row, half] = jnp.where((field == 2) | (field == 3), value, 0.0)

    def across(pair, step):
        turned = [roll(value, -step, 1) for value in pair]
        edge = lane >= LANES - step if step > 0 else lane < -step
        return jnp.where(edge, turned[1], turned[0]), jnp.where(edge, turned[0], turned[1])

    def both(ref, row):
        return ref[row, 0], ref[row, 1]

    def gather(total, value, entry):
        _, at, width = entry
        turned = roll(value, at + width, 1)
        return jnp.where((lane >= at) & (lane < at + 2 * width), turned, total)

    def scatter(value, entry):
        _, at, width = entry
        turned = roll(value, -(at + width), 1)
        return jnp.where((lane < width) | (lane >= LANES - width), turned, 0.0)

    def tile_lanes(tile):
        return slice(tile * LANES, (tile + 1) * LANES)

    gravity = jnp.where(field == 5, -GRAV, 0.0)
    keep = jnp.where(speed, DAMP, 1.0)

    def forward(k, state, target):
        plan = PLANS[k]
        x_ref = xs[k]
        moved = span((8, 6, 0)[k])
        packed = {tile: [zero, zero] for tile in plan.packed}
        for row in sorted(set(moved) | set(span(plan.reach))):
            here, up, down = both(state, row), both(state, row + 1), both(state, row - 1)
            right, left = across(here, 1), across(here, -1)
            update = row in moved
            if update:
                up2, down2 = both(state, row + 2), both(state, row - 2)
                right2, left2 = across(here, 2), across(here, -2)
            for half in range(2):
                s = here[half]
                twice = 2.0 * s
                lap_rows = up[half] + down[half] - twice
                lap_columns = right[half] + left[half] - twice
                slope_rows = 0.5 * (up[half] - down[half])
                slope_columns = 0.5 * (right[half] - left[half])
                if row in plan.tile:
                    mixed = jnp.where(field == 0, slope_rows, sign_ref[row, half])
                    mixed = jnp.where(field == 1, slope_columns, mixed)
                    mixed = jnp.where(field == 6, lap_rows, mixed)
                    mixed = jnp.where(field == 7, lap_columns, mixed)
                    if half == 0:
                        x_ref[:, tile_lanes(plan.tile[row])] = jnp.concatenate([s, mixed], axis=0).astype(BF16)
                    else:
                        for table in (plan.forward, plan.backward):
                            if row in table and (table is plan.forward or table[row] != plan.forward.get(row)):
                                entry = table[row]
                                old = packed[entry[0]]
                                packed[entry[0]] = [gather(old[0], s, entry), gather(old[1], mixed, entry)]
                if update and (half == 0 or k < 2):
                    bend = (up2[half] + down2[half] + right2[half] + left2[half]) - 4.0 * (
                        up[half] + down[half] + right[half] + left[half]
                    )
                    bend = bend + 12.0 * s
                    pull = k0_ref[row, half] * lap_rows + k1_ref[row, half] * lap_columns - KB * bend
                    turn = KC * jnp.where(field == 6, slope_rows, jnp.where(field == 7, slope_columns, 0.0))
                    force = roll(pull, 3, 0) + roll(turn, 5, 0) + gravity
                    rate = KS * jnp.where(field == 6, lap_rows, lap_columns)
                    change = jnp.where(speed, force, jnp.where(slide, rate, 0.0))
                    later[row, half] = keep * s + DT * change
        for tile, (top, bottom) in packed.items():
            x_ref[:, tile_lanes(tile)] = jnp.concatenate([top, bottom], axis=0).astype(BF16)

        def layer(z, keep_slope, block):
            bent = jnp.tanh(z)
            part = z * bent
            start, stop = block[0] * LANES, min(block[1], plan.saved) * LANES
            if stop > start:
                keep_slope[start:stop, :] = (1.0 + bent) * (1.0 + (z - part))
            return (z + part).astype(BF16)

        for block in plan.blocks:
            at = slice(block[0] * LANES, block[1] * LANES)
            act = layer(dot_columns(x_ref[:, at], w1_half), slopes_first[k], block)
            if block[0] == 0:
                act_first[k] = act
            act = layer(dot(act, w2), slopes_second[k], block)
            if block[0] == 0:
                act_second[k] = act
            if k < 2 or block[0] == 0:
                friction[:, at] = dot_rows(w3t, act)
        for row in moved:
            for half in range(2 if k < 2 else 1):
                value = later[row, half]
                if half == 0 and row in plan.tile:
                    value = value - DT * friction[:, tile_lanes(plan.tile[row])]
                if half == 1 and row in plan.forward:
                    entry = plan.forward[row]
                    value = value - DT * scatter(friction[:, tile_lanes(entry[0])], entry)
                value = mask_ref[row, half] * value
                value = value + jnp.where(place, DT * roll(value, 5, 0), 0.0)
                if k < 2:
                    target[row, half] = value
                else:
                    final_ref[0, :, row - FIRST, :] = value

    forward(0, state_a, state_b)
    forward(1, state_b, state_a)
    forward(2, state_a, None)
    final_copy = pltpu.make_async_copy(final_ref, final_hbm, sems.at[0])
    final_copy.start()

    def backward(k):
        plan = PLANS[k]
        inner, middle, outer = plan.back - 1, plan.back, plan.back + 1
        packed = zero
        for row in span(middle):
            for half in range(2):
                value = jnp.where(slide, -DT * adjoint[row, half], 0.0)
                if half == 0:
                    upstream[:, tile_lanes(plan.tile[row])] = jnp.concatenate([value, zero], axis=0).astype(BF16)
                elif row in plan.backward:
                    packed = gather(packed, value, plan.backward[row])
        upstream[:, tile_lanes(plan.near)] = jnp.concatenate([packed, zero], axis=0).astype(BF16)
        for start, stop in ((0, TILE_ROWS), (TILE_ROWS, plan.near + 1)):
            at = slice(start * LANES, stop * LANES)
            second_back = (dot_columns(upstream[:, at], w3) * slopes_second[k][at, :]).astype(BF16)
            first_back = (dot_rows(second_back, w2) * slopes_first[k][at, :]).astype(BF16)
            feature_back[:, at] = dot_rows(w1, first_back)
            if start == 0:
                second = dot_columns(act_first[k], second_back)
                first = dot(xs[k][:, at], first_back)
                third = dot(upstream[:, at], act_second[k])
        if k == 2:
            total_second[...], total_first[...], total_third[...] = second, first, third
        else:
            total_second[...] += second
            total_first[...] += first
            total_third[...] += third

        for row in span(outer):
            for half in range(2):
                q = adjoint[row, half]
                total = mask_ref[row, half] * (q + DT * roll(q, 3, 0))
                force_ref[row, half] = jnp.where(place, DT * roll(total, 5, 0), 0.0)
                if distance(row) <= inner:
                    sum_ref[row, half] = jnp.where(speed, DAMP * total, q)
        for row in span(middle):
            force = both(force_ref, row)
            high, low = [], []
            for half in range(2):
                q, g = adjoint[row, half], force[half]
                if half == 0:
                    at = tile_lanes(plan.tile[row])
                    straight, mixed = feature_back[0:8, at], feature_back[8:16, at]
                elif row in plan.backward:
                    entry = plan.backward[row]
                    at = tile_lanes(entry[0])
                    straight, mixed = scatter(feature_back[0:8, at], entry), scatter(feature_back[8:16, at], entry)
                else:
                    straight, mixed = zero, zero
                carried = DT * KS * q + mixed
                by_rows = k0_ref[row, half] * g + jnp.where(field == 6, carried, 0.0)
                by_columns = k1_ref[row, half] * g + jnp.where(field == 7, carried, 0.0)
                tilt = 0.5 * jnp.where(slide, KC * roll(g, 6, 0), mixed)
                tilt_rows = jnp.where((field == 0) | (field == 6), tilt, 0.0)
                tilt_columns = jnp.where((field == 1) | (field == 7), tilt, 0.0)
                ahead_ref[row, half] = by_rows + 4.0 * KB * g - tilt_rows
                behind_ref[row, half] = by_rows + 4.0 * KB * g + tilt_rows
                high.append(by_columns + 4.0 * KB * g - tilt_columns)
                low.append(by_columns + 4.0 * KB * g + tilt_columns)
                if distance(row) <= inner:
                    center = -2.0 * (by_rows + by_columns) - 12.0 * KB * g
                    sum_ref[row, half] = sum_ref[row, half] + straight + center
            if distance(row) <= inner:
                right, left = across(high, 1), across(low, -1)
                right2, left2 = across(force, 2), across(force, -2)
                for half in range(2):
                    sideways = right[half] + left[half] - KB * (right2[half] + left2[half])
                    sum_ref[row, half] = sum_ref[row, half] + sideways
        for row in span(inner):
            for half in range(2 if k > 0 else 1):
                value = sum_ref[row, half] + ahead_ref[row + 1, half] + behind_ref[row - 1, half]
                value = value - KB * (force_ref[row + 2, half] + force_ref[row - 2, half])
                if k > 0:
                    adjoint[row, half] = jnp.where(slide, mask_ref[row, half] * value, value)
                else:
                    adjoint_ref[0, :, row - FIRST, :] = value

    backward(2)
    backward(1)
    backward(0)
    adjoint_copy = pltpu.make_async_copy(adjoint_ref, adjoint_hbm, sems.at[1])
    adjoint_copy.start()

    small = total_first[...]
    third = total_third[0:8, :]
    row_index = lax.broadcasted_iota(jnp.int32, (8, HID), 0)
    top = jnp.where(row_index < 2, pltpu.roll(third, 2, 0), small[0:8])
    bottom = small[8:16]
    for c in range(HID // 8):
        for j in range(8):
            at = 8 * c + (2 * j) % 8
            side = slice(0, LANES) if j < 4 else slice(LANES, HID)
            grads_ref[c, j] = total_second[at : at + 2, side]
        line = (top if c < 16 else bottom)[(c // 2) % 8 : (c // 2) % 8 + 1, (c % 2) * LANES : (c % 2 + 1) * LANES]
        grads_ref[c, 8] = jnp.broadcast_to(line, (2, LANES))
    final_copy.wait()
    adjoint_copy.wait()


def run_main(*operands):
    rows = (ALL_ROWS, 2, 8, LANES)
    scratch = [pltpu.VMEM((1, 8, TILE_ROWS, LANES), F32)] * 2 + [pltpu.SemaphoreType.DMA((2,))]
    scratch += [pltpu.VMEM(rows, F32) for _ in range(12)]
    scratch += [pltpu.VMEM((16, plan.tiles * LANES), BF16) for plan in PLANS]
    scratch += [pltpu.VMEM((plan.saved * LANES, HID), F32) for plan in PLANS] * 2
    scratch += [pltpu.VMEM((3, OWN, HID), BF16)] * 2
    scratch += [
        pltpu.VMEM((8, PLANS[0].tiles * LANES), F32),
        pltpu.VMEM((16, PLANS[2].tiles * LANES), BF16),
        pltpu.VMEM((16, PLANS[2].tiles * LANES), F32),
        pltpu.VMEM((HID, HID), F32),
        pltpu.VMEM((16, HID), F32),
        pltpu.VMEM((16, HID), F32),
    ]
    return pl.pallas_call(
        main_kernel,
        out_shape=(
            jax.ShapeDtypeStruct((1, 8, TILE_ROWS, LANES), F32),
            jax.ShapeDtypeStruct((1, 8, TILE_ROWS, LANES), F32),
            jax.ShapeDtypeStruct((HID // 8, 9, 2, LANES), F32),
        ),
        in_specs=[pl.BlockSpec(memory_space=pltpu.SMEM if i == 1 else pltpu.VMEM) for i in range(len(operands))],
        out_specs=[pl.BlockSpec(memory_space=m) for m in (pltpu.HBM, pltpu.HBM, pltpu.VMEM)],
        scratch_shapes=scratch,
        compiler_params=pltpu.CompilerParams(vmem_limit_bytes=40 << 20),
        name="substeps",
    )(*operands)


def run_pack(*operands):
    return pl.pallas_call(
        pack_kernel,
        out_shape=(
            jax.ShapeDtypeStruct((TILE_ROWS, 24, LANES), F32),
            jax.ShapeDtypeStruct((24, LANES), F32),
            jax.ShapeDtypeStruct((24, LANES), F32),
            jax.ShapeDtypeStruct((1, 24, LANES), F32),
        ),
        in_specs=[pl.BlockSpec(memory_space=pltpu.HBM)] * 6,
        scratch_shapes=[pltpu.VMEM(value.shape, value.dtype) for value in operands]
        + [pltpu.SemaphoreType.DMA((6,))],
        name="pack_tile",
    )(*operands)


def shift(value, axis, step):
    count = lax.axis_size(axis)
    return lax.ppermute(value, axis, [(i, i + step) for i in range(count) if 0 <= i + step < count])


def sum_everywhere(part):
    plane, column = lax.axis_size(PLANE), lax.axis_size(COLUMN)
    part = jnp.sum(lax.all_to_all(part, PLANE, 0, 0, tiled=True), axis=0)
    part = jnp.broadcast_to(part, (column,) + part.shape)
    part = jnp.sum(lax.all_to_all(part, COLUMN, 0, 0, tiled=True), axis=0)
    part = jnp.broadcast_to(part, (plane,) + part.shape)
    return lax.all_to_all(part, PLANE, 0, 0, tiled=True)


def finish_kernel(scale, flat_ref, first_ref, second_ref, third_ref):
    for c in range(HID // 8):
        for j in range(8):
            at = 8 * c + (2 * j) % 8
            side = slice(0, LANES) if j < 4 else slice(LANES, HID)
            second_ref[at : at + 2, side] = flat_ref[c, j] * scale
    for half in range(2):
        at = slice(half * LANES, (half + 1) * LANES)
        for f, row in enumerate(FEATURE_ROWS):
            first_ref[f : f + 1, at] = flat_ref[2 * row + half, 8, 0:1, :] * scale
        for f in range(2):
            third_ref[f : f + 1, at] = flat_ref[2 * f + half, 8, 0:1, :] * scale


def shards(state, adjoint, stiffness, pinned, weave, first_weight, second_weight, third_weight):
    own, low_edge, high_edge, last = run_pack(state, adjoint, stiffness, pinned, weave, third_weight.T)
    left = shift(high_edge, WEFT, 1)
    right = shift(low_edge, WEFT, -1)
    own = jnp.concatenate([own, left[None], right[None], last], axis=0)
    count = lax.axis_size(WARP)
    core = lax.axis_index(WARP) % 2
    mates = [(i, i ^ 1) for i in range(count)]
    partner = lax.ppermute(own, WARP, mates)
    outward = lax.dynamic_slice_in_dim(partner, core * (TILE_ROWS - 2), 2, axis=0)[:, 0:8]
    tail = jnp.concatenate([outward, partner[TILE_ROWS : TILE_ROWS + 2, 0:8], jnp.zeros((2, 8, LANES), F32)], axis=0)
    wide = jnp.concatenate([own[: TILE_ROWS + 2], tail.reshape(2, 24, LANES)], axis=0)
    pairs = [(i, j) for i in range(count) for j in [((i + 1) ^ 1) - 1] if 0 <= j < count]
    cross = lax.ppermute(wide, WARP, pairs)
    inward = lax.dynamic_slice_in_dim(cross, (1 - core) * (TILE_ROWS - 2), 2, axis=0)[:, 0:8]
    far = lax.ppermute(jnp.concatenate([inward, cross[TILE_ROWS : TILE_ROWS + 2, 0:8]], axis=0), WARP, mates)

    final_state, state_adjoint, grads = run_main(
        own, core.reshape(1), partner, cross, far, first_weight, second_weight
    )
    flat = sum_everywhere(grads)
    cells = OWN * lax.axis_size(WARP) * lax.axis_size(WEFT)
    first, second, third = pl.pallas_call(
        functools.partial(finish_kernel, float(cells) ** -0.5),
        out_shape=(
            jax.ShapeDtypeStruct((12, HID), F32),
            jax.ShapeDtypeStruct((HID, HID), F32),
            jax.ShapeDtypeStruct((2, HID), F32),
        ),
        compiler_params=pltpu.CompilerParams(vmem_limit_bytes=4 << 20),
        name="unpack_grads",
    )(flat)
    return final_state, state_adjoint, first, second, third.T


def factors(mesh):
    warp, weft = mesh.shape["warp"], mesh.shape["weft"]
    zlo = 4 if weft % 4 == 0 else 1
    x = 4 if warp % 8 == 0 else 1
    core = 2 if warp % 2 == 0 else 1
    return (warp // (x * core), x, core, weft // zlo, zlo)


def solution(mesh):
    fine = Mesh(mesh.devices.reshape(factors(mesh)), WARP + WEFT)
    field = P(None, None, WARP, WEFT)
    placed = (field, field, P(None, WARP, WEFT), P(None, WARP, WEFT), P(WARP, WEFT), P(), P(), P())
    return jax.shard_map(
        shards,
        mesh=fine,
        in_specs=placed,
        out_specs=(field, field, P(), P(), P()),
        check_vma=False,
    )
```

```python
import functools

import jax
import jax.numpy as jnp
from jax import lax
from jax.experimental import pallas as pl
from jax.experimental.pallas import tpu as pltpu
from jax.sharding import Mesh, PartitionSpec as P

WARP = ("zhi", "x", "core")
WEFT = ("y", "zlo")
PLANE = ("x", "core", "y")
COLUMN = ("zhi", "zlo")

DT = 0.25
DAMP = 0.9
KB = 0.25
KC = 0.5
KS = 0.5
GRAV = 0.3

TILE_ROWS = 8
LANES = 128
REACH = 10
FIRST = REACH
ALL_ROWS = TILE_ROWS + 2 * REACH
HID = 256
OWN = TILE_ROWS * LANES
FEATURE_ROWS = (6, 7, 3, 4, 5, 14, 15, 8, 9, 2, 10, 11)
F32 = jnp.float32
BF16 = jnp.bfloat16


def span(radius):
    return range(FIRST - radius, FIRST + TILE_ROWS + radius)


def distance(row):
    return max(FIRST - row, row - (FIRST + TILE_ROWS - 1), 0)


def ring(e):
    return [FIRST - e, FIRST + TILE_ROWS - 1 + e]


class Plan:
    def __init__(self, reach, back):
        self.reach, self.back = reach, back
        own = list(range(FIRST, FIRST + TILE_ROWS))
        order = own + [r for e in range(1, back + 1) for r in ring(e)]
        near = len(order)
        order = order + [None] + [r for e in range(back + 1, reach + 1) for r in ring(e)]
        self.tile = {r: t for t, r in enumerate(order) if r is not None}
        self.forward, self.backward = {}, {}
        at = {near: 0, len(order): 0}

        def put(table, row, tile, width):
            table[row] = (tile, at[tile], width)
            at[tile] += 2 * width

        for r in own:
            put(self.forward, r, near, reach)
            self.backward[r] = self.forward[r]
        for e in range(1, reach):
            width, need = reach - e, back - e
            for r in ring(e):
                if need > 0 and at[near] + 2 * width <= LANES and (e == 1 or reach == back):
                    put(self.forward, r, near, width)
                    self.backward[r] = self.forward[r]
                else:
                    put(self.forward, r, len(order), width)
                    if need > 0:
                        put(self.backward, r, near, need)
        self.packed = {near} | ({len(order)} if at[len(order)] else set())
        assert max(at.values()) <= LANES
        self.near = near
        self.tiles = len(order) + (1 if at[len(order)] else 0)
        middle = {16: 16, 14: 15}.get(self.tiles - TILE_ROWS, self.tiles)
        self.saved = middle
        self.blocks = [(0, TILE_ROWS), (TILE_ROWS, middle)]
        if middle < self.tiles:
            self.blocks.append((middle, self.tiles))


PLANS = [Plan(7, 1), Plan(6, 3), Plan(5, 5)]


def dot(left, right):
    return lax.dot_general(left, right, (((1,), (0,)), ((), ())), preferred_element_type=F32)


def dot_columns(left, right):
    return lax.dot_general(left, right, (((0,), (0,)), ((), ())), preferred_element_type=F32)


def dot_rows(left, right):
    return lax.dot_general(left, right, (((1,), (1,)), ((), ())), preferred_element_type=F32)


def lane_index():
    return lax.broadcasted_iota(jnp.int32, (8, LANES), 1)


def field_index():
    return lax.broadcasted_iota(jnp.int32, (8, LANES), 0)


def pack_kernel(
    state_hbm, adjoint_hbm, stiff_hbm, pinned_hbm, weave_hbm, third_hbm,
    own_ref, low_ref, high_ref, last_ref,
    state_ref, adjoint_ref, stiff_ref, pinned_ref, weave_ref, third_ref, sems,
):
    sources = (state_hbm, adjoint_hbm, stiff_hbm, pinned_hbm, weave_hbm, third_hbm)
    targets = (state_ref, adjoint_ref, stiff_ref, pinned_ref, weave_ref, third_ref)
    copies = [pltpu.make_async_copy(a, b, sems.at[i]) for i, (a, b) in enumerate(zip(sources, targets))]
    for copy in copies:
        copy.start()
    for copy in copies:
        copy.wait()
    lane, field = lane_index(), field_index()
    last_ref[...] = jnp.zeros((1, 24, LANES), F32)
    third = third_ref[...].astype(F32)
    for f in range(2):
        last_ref[0, 2 * f : 2 * f + 1, :] = third[f : f + 1, 0:LANES]
        last_ref[0, 2 * f + 1 : 2 * f + 2, :] = third[f : f + 1, LANES:]
    low = [jnp.zeros((8, LANES), F32) for _ in range(3)]
    high = [jnp.zeros((8, LANES), F32) for _ in range(3)]
    for row in range(TILE_ROWS):
        k0 = stiff_ref[0, row : row + 1, :]
        k1 = stiff_ref[1, row : row + 1, :]
        free = 1.0 - pinned_ref[0, row : row + 1, :].astype(F32)
        code = weave_ref[row : row + 1, :]
        first_sign = (2 * jnp.bitwise_and(code, 1) - 1).astype(F32)
        second_sign = (2 * jnp.right_shift(code, 1) - 1).astype(F32)
        cell = jnp.where(field == 5, 1.0, 0.0)
        for place, value in enumerate((k0, k1, first_sign, second_sign, free)):
            cell = jnp.where(field == place, value, cell)
        at = REACH * row
        here = (lane >= at) & (lane < at + REACH)
        for part, value in enumerate((state_ref[0, :, row, :], adjoint_ref[0, :, row, :], cell)):
            own_ref[row, 8 * part : 8 * part + 8, :] = value
            low[part] = jnp.where(here, pltpu.roll(value, at, 1) if at else value, low[part])
            shift = (at + REACH) % LANES
            high[part] = jnp.where(here, pltpu.roll(value, shift, 1), high[part])
    for part in range(3):
        low_ref[8 * part : 8 * part + 8, :] = low[part]
        high_ref[8 * part : 8 * part + 8, :] = high[part]


def roll(value, shift, axis):
    shift = shift % value.shape[axis]
    return pltpu.roll(value, shift, axis) if shift else value


def main_kernel(
    own_ref,
    core_ref,
    partner_ref,
    cross_ref,
    far_ref,
    first_weight_ref,
    second_weight_ref,
    final_hbm,
    adjoint_hbm,
    grads_ref,
    final_ref,
    adjoint_ref,
    sems,
    state_a,
    state_b,
    later,
    adjoint,
    k0_ref,
    k1_ref,
    mask_ref,
    sign_ref,
    force_ref,
    ahead_ref,
    behind_ref,
    sum_ref,
    x0,
    x1,
    x2,
    slope_first0,
    slope_first1,
    slope_first2,
    slope_second0,
    slope_second1,
    slope_second2,
    act_first,
    act_second,
    friction,
    upstream,
    feature_back,
    total_second,
    total_first,
    total_third,
):
    lane, field = lane_index(), field_index()
    zero = jnp.zeros((8, LANES), F32)
    xs = (x0, x1, x2)
    slopes_first = (slope_first0, slope_first1, slope_first2)
    slopes_second = (slope_second0, slope_second1, slope_second2)
    f_row = lax.broadcasted_iota(jnp.int32, (16, 12), 0)
    f_column = lax.broadcasted_iota(jnp.int32, (16, 12), 1)
    chosen = jnp.zeros((16, 12), F32)
    for f, n in enumerate(FEATURE_ROWS):
        chosen = jnp.where((f_row == n) & (f_column == f), 1.0, chosen)
    w1_wide = dot(chosen.astype(BF16), first_weight_ref[...])
    w1, w1_half = w1_wide.astype(BF16), (0.5 * w1_wide).astype(BF16)
    w2 = (0.5 * second_weight_ref[...].astype(F32)).astype(BF16)
    f_row = lax.broadcasted_iota(jnp.int32, (16, 2), 0)
    f_column = lax.broadcasted_iota(jnp.int32, (16, 2), 1)
    third = [
        jnp.concatenate([own_ref[TILE_ROWS + 2, 2 * f + i : 2 * f + i + 1, :] for i in range(2)], axis=1)
        for f in range(2)
    ]
    third = jnp.concatenate(third, axis=0).astype(BF16)
    w3_wide = dot(jnp.where(f_row == f_column + 6, 1.0, 0.0).astype(BF16), third)
    w3t, w3 = w3_wide[0:8].astype(BF16), (0.5 * w3_wide).astype(BF16)
    place = field < 3
    speed = (field >= 3) & (field < 6)
    slide = field >= 6

    def beside(low, high, row):
        at = REACH * row
        out = jnp.where(lane < REACH, roll(high, -at, 1), 0.0)
        return jnp.where(lane >= LANES - REACH, roll(low, LANES - REACH - at, 1), out)

    first_core = core_ref[0] == 0

    def pick(lower, upper, at):
        return jnp.where(first_core, lower[at], upper[at])

    def received(e, part):
        at = slice(8 * part, 8 * part + 8)
        if e < -TILE_ROWS:
            i = e + TILE_ROWS + 2
            return [
                jnp.where(first_core, cross_ref[n, p, :], far_ref[m])
                for (n, p), m in zip(extra(i), (i, 2, 3))
            ]
        if e < 0:
            return [pick(cross_ref, partner_ref, (i, at)) for i in (e + TILE_ROWS, TILE_ROWS, TILE_ROWS + 1)]
        if e < TILE_ROWS:
            return [own_ref[i, at, :] for i in (e, TILE_ROWS, TILE_ROWS + 1)]
        if e < 2 * TILE_ROWS:
            return [pick(partner_ref, cross_ref, (i, at)) for i in (e - TILE_ROWS, TILE_ROWS, TILE_ROWS + 1)]
        i = e - 2 * TILE_ROWS
        return [
            jnp.where(first_core, far_ref[m], cross_ref[n, p, :])
            for (n, p), m in zip(extra(i), (i, 2, 3))
        ]

    def extra(i):
        n = TILE_ROWS + 2
        row = (n, slice(8 * i, 8 * i + 8))
        return row, (n, slice(16, 24)), (n + 1, slice(0, 8))

    for row in range(ALL_ROWS):
        e = row - FIRST
        near = e % TILE_ROWS
        for part in range(3 if -TILE_ROWS <= e < 2 * TILE_ROWS else 1):
            value, low, high = received(e, part)
            pair = (value, beside(low, high, near))
            for half in range(2):
                value = pair[half]
                if part == 0:
                    state_a[row, half] = value
                elif part == 1:
                    adjoint[row, half] = value
                else:
                    k0_ref[row, half] = jnp.broadcast_to(value[0:1], (8, LANES))
                    k1_ref[row, half] = jnp.broadcast_to(value[1:2], (8, LANES))
                    mask_ref[row, half] = jnp.where(
                        place, 1.0, jnp.where(speed, value[4:5], value[5:6])
                    )
                    sign_ref[row, half] = jnp.where((field == 2) | (field == 3), value, 0.0)

    def across(pair, step):
        turned = [roll(value, -step, 1) for value in pair]
        edge = lane >= LANES - step if step > 0 else lane < -step
        return jnp.where(edge, turned[1], turned[0]), jnp.where(edge, turned[0], turned[1])

    def both(ref, row):
        return ref[row, 0], ref[row, 1]

    def gather(total, value, entry):
        _, at, width = entry
        turned = roll(value, at + width, 1)
        return jnp.where((lane >= at) & (lane < at + 2 * width), turned, total)

    def scatter(value, entry):
        _, at, width = entry
        turned = roll(value, -(at + width), 1)
        return jnp.where((lane < width) | (lane >= LANES - width), turned, 0.0)

    def tile_lanes(tile):
        return slice(tile * LANES, (tile + 1) * LANES)

    gravity = jnp.where(field == 5, -GRAV, 0.0)
    keep = jnp.where(speed, DAMP, 1.0)

    def forward(k, state, target):
        plan = PLANS[k]
        x_ref = xs[k]
        moved = span((8, 6, 0)[k])
        packed = {tile: [zero, zero] for tile in plan.packed}
        for row in sorted(set(moved) | set(span(plan.reach))):
            here, up, down = both(state, row), both(state, row + 1), both(state, row - 1)
            right, left = across(here, 1), across(here, -1)
            update = row in moved
            if update:
                up2, down2 = both(state, row + 2), both(state, row - 2)
                right2, left2 = across(here, 2), across(here, -2)
            for half in range(2):
                s = here[half]
                twice = 2.0 * s
                lap_rows = up[half] + down[half] - twice
                lap_columns = right[half] + left[half] - twice
                slope_rows = 0.5 * (up[half] - down[half])
                slope_columns = 0.5 * (right[half] - left[half])
                if row in plan.tile:
                    mixed = jnp.where(field == 0, slope_rows, sign_ref[row, half])
                    mixed = jnp.where(field == 1, slope_columns, mixed)
                    mixed = jnp.where(field == 6, lap_rows, mixed)
                    mixed = jnp.where(field == 7, lap_columns, mixed)
                    if half == 0:
                        x_ref[:, tile_lanes(plan.tile[row])] = jnp.concatenate([s, mixed], axis=0).astype(BF16)
                    else:
                        for table in (plan.forward, plan.backward):
                            if row in table and (table is plan.forward or table[row] != plan.forward.get(row)):
                                entry = table[row]
                                old = packed[entry[0]]
                                packed[entry[0]] = [gather(old[0], s, entry), gather(old[1], mixed, entry)]
                if update and (half == 0 or k < 2):
                    bend = (up2[half] + down2[half] + right2[half] + left2[half]) - 4.0 * (
                        up[half] + down[half] + right[half] + left[half]
                    )
                    bend = bend + 12.0 * s
                    pull = k0_ref[row, half] * lap_rows + k1_ref[row, half] * lap_columns - KB * bend
                    turn = KC * jnp.where(field == 6, slope_rows, jnp.where(field == 7, slope_columns, 0.0))
                    force = roll(pull, 3, 0) + roll(turn, 5, 0) + gravity
                    rate = KS * jnp.where(field == 6, lap_rows, lap_columns)
                    change = jnp.where(speed, force, jnp.where(slide, rate, 0.0))
                    later[row, half] = keep * s + DT * change
        for tile, (top, bottom) in packed.items():
            x_ref[:, tile_lanes(tile)] = jnp.concatenate([top, bottom], axis=0).astype(BF16)

        def layer(z, keep_slope, block):
            bent = jnp.tanh(z)
            part = z * bent
            start, stop = block[0] * LANES, min(block[1], plan.saved) * LANES
            if stop > start:
                keep_slope[start:stop, :] = (1.0 + bent) * (1.0 + (z - part))
            return (z + part).astype(BF16)

        for block in plan.blocks:
            at = slice(block[0] * LANES, block[1] * LANES)
            act = layer(dot_columns(x_ref[:, at], w1_half), slopes_first[k], block)
            if block[0] == 0:
                act_first[k] = act
            act = layer(dot(act, w2), slopes_second[k], block)
            if block[0] == 0:
                act_second[k] = act
            if k < 2 or block[0] == 0:
                friction[:, at] = dot_rows(w3t, act)
        for row in moved:
            for half in range(2 if k < 2 else 1):
                value = later[row, half]
                if half == 0 and row in plan.tile:
                    value = value - DT * friction[:, tile_lanes(plan.tile[row])]
                if half == 1 and row in plan.forward:
                    entry = plan.forward[row]
                    value = value - DT * scatter(friction[:, tile_lanes(entry[0])], entry)
                value = mask_ref[row, half] * value
                value = value + jnp.where(place, DT * roll(value, 5, 0), 0.0)
                if k < 2:
                    target[row, half] = value
                else:
                    final_ref[0, :, row - FIRST, :] = value

    forward(0, state_a, state_b)
    forward(1, state_b, state_a)
    forward(2, state_a, None)
    final_copy = pltpu.make_async_copy(final_ref, final_hbm, sems.at[0])
    final_copy.start()

    def backward(k):
        plan = PLANS[k]
        inner, middle, outer = plan.back - 1, plan.back, plan.back + 1
        packed = zero
        for row in span(middle):
            for half in range(2):
                value = jnp.where(slide, -DT * adjoint[row, half], 0.0)
                if half == 0:
                    upstream[:, tile_lanes(plan.tile[row])] = jnp.concatenate([value, zero], axis=0).astype(BF16)
                elif row in plan.backward:
                    packed = gather(packed, value, plan.backward[row])
        upstream[:, tile_lanes(plan.near)] = jnp.concatenate([packed, zero], axis=0).astype(BF16)
        for start, stop in ((0, TILE_ROWS), (TILE_ROWS, plan.near + 1)):
            at = slice(start * LANES, stop * LANES)
            second_back = (dot_columns(upstream[:, at], w3) * slopes_second[k][at, :]).astype(BF16)
            first_back = (dot_rows(second_back, w2) * slopes_first[k][at, :]).astype(BF16)
            feature_back[:, at] = dot_rows(w1, first_back)
            if start == 0:
                second = dot_columns(act_first[k], second_back)
                first = dot(xs[k][:, at], first_back)
                third = dot(upstream[:, at], act_second[k])
        if k == 2:
            total_second[...], total_first[...], total_third[...] = second, first, third
        else:
            total_second[...] += second
            total_first[...] += first
            total_third[...] += third

        for row in span(outer):
            for half in range(2):
                q = adjoint[row, half]
                total = mask_ref[row, half] * (q + DT * roll(q, 3, 0))
                force_ref[row, half] = jnp.where(place, DT * roll(total, 5, 0), 0.0)
                if distance(row) <= inner:
                    sum_ref[row, half] = jnp.where(speed, DAMP * total, q)
        for row in span(middle):
            force = both(force_ref, row)
            high, low = [], []
            for half in range(2):
                q, g = adjoint[row, half], force[half]
                if half == 0:
                    at = tile_lanes(plan.tile[row])
                    straight, mixed = feature_back[0:8, at], feature_back[8:16, at]
                elif row in plan.backward:
                    entry = plan.backward[row]
                    at = tile_lanes(entry[0])
                    straight, mixed = scatter(feature_back[0:8, at], entry), scatter(feature_back[8:16, at], entry)
                else:
                    straight, mixed = zero, zero
                carried = DT * KS * q + mixed
                by_rows = k0_ref[row, half] * g + jnp.where(field == 6, carried, 0.0)
                by_columns = k1_ref[row, half] * g + jnp.where(field == 7, carried, 0.0)
                tilt = 0.5 * jnp.where(slide, KC * roll(g, 6, 0), mixed)
                tilt_rows = jnp.where((field == 0) | (field == 6), tilt, 0.0)
                tilt_columns = jnp.where((field == 1) | (field == 7), tilt, 0.0)
                ahead_ref[row, half] = by_rows + 4.0 * KB * g - tilt_rows
                behind_ref[row, half] = by_rows + 4.0 * KB * g + tilt_rows
                high.append(by_columns + 4.0 * KB * g - tilt_columns)
                low.append(by_columns + 4.0 * KB * g + tilt_columns)
                if distance(row) <= inner:
                    center = -2.0 * (by_rows + by_columns) - 12.0 * KB * g
                    sum_ref[row, half] = sum_ref[row, half] + straight + center
            if distance(row) <= inner:
                right, left = across(high, 1), across(low, -1)
                right2, left2 = across(force, 2), across(force, -2)
                for half in range(2):
                    sideways = right[half] + left[half] - KB * (right2[half] + left2[half])
                    sum_ref[row, half] = sum_ref[row, half] + sideways
        for row in span(inner):
            for half in range(2 if k > 0 else 1):
                value = sum_ref[row, half] + ahead_ref[row + 1, half] + behind_ref[row - 1, half]
                value = value - KB * (force_ref[row + 2, half] + force_ref[row - 2, half])
                if k > 0:
                    adjoint[row, half] = jnp.where(slide, mask_ref[row, half] * value, value)
                else:
                    adjoint_ref[0, :, row - FIRST, :] = value

    backward(2)
    backward(1)
    backward(0)
    adjoint_copy = pltpu.make_async_copy(adjoint_ref, adjoint_hbm, sems.at[1])
    adjoint_copy.start()

    small = total_first[...]
    third = total_third[0:8, :]
    row_index = lax.broadcasted_iota(jnp.int32, (8, HID), 0)
    top = jnp.where(row_index < 2, pltpu.roll(third, 2, 0), small[0:8])
    bottom = small[8:16]
    for c in range(HID // 8):
        for j in range(8):
            at = 8 * c + (2 * j) % 8
            side = slice(0, LANES) if j < 4 else slice(LANES, HID)
            grads_ref[c, j] = total_second[at : at + 2, side]
        line = (top if c < 16 else bottom)[(c // 2) % 8 : (c // 2) % 8 + 1, (c % 2) * LANES : (c % 2 + 1) * LANES]
        grads_ref[c, 8] = jnp.broadcast_to(line, (2, LANES))
    final_copy.wait()
    adjoint_copy.wait()


def run_main(*operands):
    rows = (ALL_ROWS, 2, 8, LANES)
    scratch = [pltpu.VMEM((1, 8, TILE_ROWS, LANES), F32)] * 2 + [pltpu.SemaphoreType.DMA((2,))]
    scratch += [pltpu.VMEM(rows, F32) for _ in range(12)]
    scratch += [pltpu.VMEM((16, plan.tiles * LANES), BF16) for plan in PLANS]
    scratch += [pltpu.VMEM((plan.saved * LANES, HID), F32) for plan in PLANS] * 2
    scratch += [pltpu.VMEM((3, OWN, HID), BF16)] * 2
    scratch += [
        pltpu.VMEM((8, PLANS[0].tiles * LANES), F32),
        pltpu.VMEM((16, PLANS[2].tiles * LANES), BF16),
        pltpu.VMEM((16, PLANS[2].tiles * LANES), F32),
        pltpu.VMEM((HID, HID), F32),
        pltpu.VMEM((16, HID), F32),
        pltpu.VMEM((16, HID), F32),
    ]
    return pl.pallas_call(
        main_kernel,
        out_shape=(
            jax.ShapeDtypeStruct((1, 8, TILE_ROWS, LANES), F32),
            jax.ShapeDtypeStruct((1, 8, TILE_ROWS, LANES), F32),
            jax.ShapeDtypeStruct((HID // 8, 9, 2, LANES), F32),
        ),
        in_specs=[pl.BlockSpec(memory_space=pltpu.SMEM if i == 1 else pltpu.VMEM) for i in range(len(operands))],
        out_specs=[pl.BlockSpec(memory_space=m) for m in (pltpu.HBM, pltpu.HBM, pltpu.VMEM)],
        scratch_shapes=scratch,
        compiler_params=pltpu.CompilerParams(vmem_limit_bytes=40 << 20),
        name="substeps",
    )(*operands)


def run_pack(*operands):
    return pl.pallas_call(
        pack_kernel,
        out_shape=(
            jax.ShapeDtypeStruct((TILE_ROWS, 24, LANES), F32),
            jax.ShapeDtypeStruct((24, LANES), F32),
            jax.ShapeDtypeStruct((24, LANES), F32),
            jax.ShapeDtypeStruct((1, 24, LANES), F32),
        ),
        in_specs=[pl.BlockSpec(memory_space=pltpu.HBM)] * 6,
        scratch_shapes=[pltpu.VMEM(value.shape, value.dtype) for value in operands]
        + [pltpu.SemaphoreType.DMA((6,))],
        compiler_params=pltpu.CompilerParams(vmem_limit_bytes=4 << 20),
        name="pack_tile",
    )(*[pltpu.with_memory_space_constraint(value, pltpu.HBM) for value in operands])


def shift(value, axis, step):
    count = lax.axis_size(axis)
    return lax.ppermute(value, axis, [(i, i + step) for i in range(count) if 0 <= i + step < count])


def sum_everywhere(part):
    plane, column = lax.axis_size(PLANE), lax.axis_size(COLUMN)
    part = jnp.sum(lax.all_to_all(part, PLANE, 0, 0, tiled=True), axis=0)
    part = jnp.broadcast_to(part, (column,) + part.shape)
    part = jnp.sum(lax.all_to_all(part, COLUMN, 0, 0, tiled=True), axis=0)
    part = jnp.broadcast_to(part, (plane,) + part.shape)
    return lax.all_to_all(part, PLANE, 0, 0, tiled=True)


def finish_kernel(scale, flat_ref, first_ref, second_ref, third_ref):
    for c in range(HID // 8):
        for j in range(8):
            at = 8 * c + (2 * j) % 8
            side = slice(0, LANES) if j < 4 else slice(LANES, HID)
            second_ref[at : at + 2, side] = flat_ref[c, j] * scale
    for half in range(2):
        at = slice(half * LANES, (half + 1) * LANES)
        for f, row in enumerate(FEATURE_ROWS):
            first_ref[f : f + 1, at] = flat_ref[2 * row + half, 8, 0:1, :] * scale
        for f in range(2):
            third_ref[f : f + 1, at] = flat_ref[2 * f + half, 8, 0:1, :] * scale


def shards(state, adjoint, stiffness, pinned, weave, first_weight, second_weight, third_weight):
    own, low_edge, high_edge, last = run_pack(state, adjoint, stiffness, pinned, weave, third_weight.T)
    left = shift(high_edge, WEFT, 1)
    right = shift(low_edge, WEFT, -1)
    own = jnp.concatenate([own, left[None], right[None], last], axis=0)
    count = lax.axis_size(WARP)
    core = lax.axis_index(WARP) % 2
    mates = [(i, i ^ 1) for i in range(count)]
    partner = lax.ppermute(own, WARP, mates)
    outward = lax.dynamic_slice_in_dim(partner, core * (TILE_ROWS - 2), 2, axis=0)[:, 0:8]
    tail = jnp.concatenate([outward, partner[TILE_ROWS : TILE_ROWS + 2, 0:8], jnp.zeros((2, 8, LANES), F32)], axis=0)
    wide = jnp.concatenate([own[: TILE_ROWS + 2], tail.reshape(2, 24, LANES)], axis=0)
    pairs = [(i, j) for i in range(count) for j in [((i + 1) ^ 1) - 1] if 0 <= j < count]
    cross = lax.ppermute(wide, WARP, pairs)
    inward = lax.dynamic_slice_in_dim(cross, (1 - core) * (TILE_ROWS - 2), 2, axis=0)[:, 0:8]
    far = lax.ppermute(jnp.concatenate([inward, cross[TILE_ROWS : TILE_ROWS + 2, 0:8]], axis=0), WARP, mates)

    final_state, state_adjoint, grads = run_main(
        own, core.reshape(1), partner, cross, far, first_weight, second_weight
    )
    flat = sum_everywhere(grads)
    cells = OWN * lax.axis_size(WARP) * lax.axis_size(WEFT)
    first, second, third = pl.pallas_call(
        functools.partial(finish_kernel, float(cells) ** -0.5),
        out_shape=(
            jax.ShapeDtypeStruct((12, HID), F32),
            jax.ShapeDtypeStruct((HID, HID), F32),
            jax.ShapeDtypeStruct((2, HID), F32),
        ),
        compiler_params=pltpu.CompilerParams(vmem_limit_bytes=4 << 20),
        name="unpack_grads",
    )(flat)
    return final_state, state_adjoint, first, second, third.T


def factors(mesh):
    warp, weft = mesh.shape["warp"], mesh.shape["weft"]
    zlo = 4 if weft % 4 == 0 else 1
    x = 4 if warp % 8 == 0 else 1
    core = 2 if warp % 2 == 0 else 1
    return (warp // (x * core), x, core, weft // zlo, zlo)


def solution(mesh):
    fine = Mesh(mesh.devices.reshape(factors(mesh)), WARP + WEFT)
    field = P(None, None, WARP, WEFT)
    placed = (field, field, P(None, WARP, WEFT), P(None, WARP, WEFT), P(WARP, WEFT), P(), P(), P())
    return jax.shard_map(
        shards,
        mesh=fine,
        in_specs=placed,
        out_specs=(field, field, P(), P(), P()),
        check_vma=False,
    )
```

```python
import functools

import jax
import jax.numpy as jnp
from jax import lax
from jax.experimental import pallas as pl
from jax.experimental.pallas import tpu as pltpu
from jax.sharding import Mesh, PartitionSpec as P

WARP = ("zhi", "x", "core")
WEFT = ("y", "zlo")
PLANE = ("x", "core", "y")
COLUMN = ("zhi", "zlo")

DT = 0.25
DAMP = 0.9
KB = 0.25
KC = 0.5
KS = 0.5
GRAV = 0.3

TILE_ROWS = 8
LANES = 128
REACH = 10
FIRST = REACH
ALL_ROWS = TILE_ROWS + 2 * REACH
HID = 256
OWN = TILE_ROWS * LANES
FEATURE_ROWS = (6, 7, 3, 4, 5, 14, 15, 8, 9, 2, 10, 11)
F32 = jnp.float32
BF16 = jnp.bfloat16


def span(radius):
    return range(FIRST - radius, FIRST + TILE_ROWS + radius)


def distance(row):
    return max(FIRST - row, row - (FIRST + TILE_ROWS - 1), 0)


def ring(e):
    return [FIRST - e, FIRST + TILE_ROWS - 1 + e]


class Plan:
    def __init__(self, reach, back):
        self.reach, self.back = reach, back
        own = list(range(FIRST, FIRST + TILE_ROWS))
        order = own + [r for e in range(1, back + 1) for r in ring(e)]
        near = len(order)
        order = order + [None] + [r for e in range(back + 1, reach + 1) for r in ring(e)]
        self.tile = {r: t for t, r in enumerate(order) if r is not None}
        self.forward, self.backward = {}, {}
        at = {near: 0, len(order): 0}

        def put(table, row, tile, width):
            table[row] = (tile, at[tile], width)
            at[tile] += 2 * width

        for r in own:
            put(self.forward, r, near, reach)
            self.backward[r] = self.forward[r]
        for e in range(1, reach):
            width, need = reach - e, back - e
            for r in ring(e):
                if need > 0 and at[near] + 2 * width <= LANES and (e == 1 or reach == back):
                    put(self.forward, r, near, width)
                    self.backward[r] = self.forward[r]
                else:
                    put(self.forward, r, len(order), width)
                    if need > 0:
                        put(self.backward, r, near, need)
        self.packed = {near} | ({len(order)} if at[len(order)] else set())
        assert max(at.values()) <= LANES
        self.near = near
        self.tiles = len(order) + (1 if at[len(order)] else 0)
        middle = {16: 16, 14: 15}.get(self.tiles - TILE_ROWS, self.tiles)
        self.saved = middle
        self.blocks = [(0, TILE_ROWS), (TILE_ROWS, middle)]
        if middle < self.tiles:
            self.blocks.append((middle, self.tiles))


PLANS = [Plan(7, 1), Plan(6, 3), Plan(5, 5)]


def dot(left, right):
    return lax.dot_general(left, right, (((1,), (0,)), ((), ())), preferred_element_type=F32)


def dot_columns(left, right):
    return lax.dot_general(left, right, (((0,), (0,)), ((), ())), preferred_element_type=F32)


def dot_rows(left, right):
    return lax.dot_general(left, right, (((1,), (1,)), ((), ())), preferred_element_type=F32)


def lane_index():
    return lax.broadcasted_iota(jnp.int32, (8, LANES), 1)


def field_index():
    return lax.broadcasted_iota(jnp.int32, (8, LANES), 0)


def pack_kernel(
    state_hbm, adjoint_hbm, stiff_hbm, pinned_hbm, weave_hbm, third_hbm,
    own_ref, low_ref, high_ref, last_ref,
    state_ref, adjoint_ref, stiff_ref, pinned_ref, weave_ref, third_ref, sems,
):
    sources = (state_hbm, adjoint_hbm, stiff_hbm, pinned_hbm, weave_hbm, third_hbm)
    targets = (state_ref, adjoint_ref, stiff_ref, pinned_ref, weave_ref, third_ref)
    copies = [pltpu.make_async_copy(a, b, sems.at[i]) for i, (a, b) in enumerate(zip(sources, targets))]
    for copy in copies:
        copy.start()
    for copy in copies:
        copy.wait()
    lane, field = lane_index(), field_index()
    last_ref[...] = jnp.zeros((1, 24, LANES), F32)
    third = third_ref[...].astype(F32)
    for f in range(2):
        last_ref[0, 2 * f : 2 * f + 1, :] = third[f : f + 1, 0:LANES]
        last_ref[0, 2 * f + 1 : 2 * f + 2, :] = third[f : f + 1, LANES:]
    low = [jnp.zeros((8, LANES), F32) for _ in range(3)]
    high = [jnp.zeros((8, LANES), F32) for _ in range(3)]
    for row in range(TILE_ROWS):
        k0 = stiff_ref[0, row : row + 1, :]
        k1 = stiff_ref[1, row : row + 1, :]
        free = 1.0 - pinned_ref[0, row : row + 1, :].astype(F32)
        code = weave_ref[row : row + 1, :]
        first_sign = (2 * jnp.bitwise_and(code, 1) - 1).astype(F32)
        second_sign = (2 * jnp.right_shift(code, 1) - 1).astype(F32)
        cell = jnp.where(field == 5, 1.0, 0.0)
        for place, value in enumerate((k0, k1, first_sign, second_sign, free)):
            cell = jnp.where(field == place, value, cell)
        at = REACH * row
        here = (lane >= at) & (lane < at + REACH)
        for part, value in enumerate((state_ref[0, :, row, :], adjoint_ref[0, :, row, :], cell)):
            own_ref[row, 8 * part : 8 * part + 8, :] = value
            low[part] = jnp.where(here, pltpu.roll(value, at, 1) if at else value, low[part])
            shift = (at + REACH) % LANES
            high[part] = jnp.where(here, pltpu.roll(value, shift, 1), high[part])
    for part in range(3):
        low_ref[8 * part : 8 * part + 8, :] = low[part]
        high_ref[8 * part : 8 * part + 8, :] = high[part]


def roll(value, shift, axis):
    shift = shift % value.shape[axis]
    return pltpu.roll(value, shift, axis) if shift else value


def main_kernel(
    own_ref,
    core_ref,
    partner_ref,
    cross_ref,
    far_ref,
    first_weight_ref,
    second_weight_ref,
    final_hbm,
    adjoint_hbm,
    grads_ref,
    final_ref,
    adjoint_ref,
    sems,
    state_a,
    state_b,
    later,
    adjoint,
    k0_ref,
    k1_ref,
    mask_ref,
    sign_ref,
    force_ref,
    ahead_ref,
    behind_ref,
    sum_ref,
    x0,
    x1,
    x2,
    slope_first0,
    slope_first1,
    slope_first2,
    slope_second0,
    slope_second1,
    slope_second2,
    act_first,
    act_second,
    friction,
    upstream,
    feature_back,
    total_second,
    total_first,
    total_third,
):
    lane, field = lane_index(), field_index()
    zero = jnp.zeros((8, LANES), F32)
    xs = (x0, x1, x2)
    slopes_first = (slope_first0, slope_first1, slope_first2)
    slopes_second = (slope_second0, slope_second1, slope_second2)
    f_row = lax.broadcasted_iota(jnp.int32, (16, 12), 0)
    f_column = lax.broadcasted_iota(jnp.int32, (16, 12), 1)
    chosen = jnp.zeros((16, 12), F32)
    for f, n in enumerate(FEATURE_ROWS):
        chosen = jnp.where((f_row == n) & (f_column == f), 1.0, chosen)
    w1_wide = dot(chosen.astype(BF16), first_weight_ref[...])
    w1, w1_half = w1_wide.astype(BF16), (0.5 * w1_wide).astype(BF16)
    w2 = (0.5 * second_weight_ref[...].astype(F32)).astype(BF16)
    f_row = lax.broadcasted_iota(jnp.int32, (16, 2), 0)
    f_column = lax.broadcasted_iota(jnp.int32, (16, 2), 1)
    third = [
        jnp.concatenate([own_ref[TILE_ROWS + 2, 2 * f + i : 2 * f + i + 1, :] for i in range(2)], axis=1)
        for f in range(2)
    ]
    third = jnp.concatenate(third, axis=0).astype(BF16)
    w3_wide = dot(jnp.where(f_row == f_column + 6, 1.0, 0.0).astype(BF16), third)
    w3t, w3 = w3_wide[0:8].astype(BF16), (0.5 * w3_wide).astype(BF16)
    place = field < 3
    speed = (field >= 3) & (field < 6)
    slide = field >= 6

    def beside(low, high, row):
        at = REACH * row
        out = jnp.where(lane < REACH, roll(high, -at, 1), 0.0)
        return jnp.where(lane >= LANES - REACH, roll(low, LANES - REACH - at, 1), out)

    first_core = core_ref[0] == 0

    def cross_at(i, part, skip):
        if i >= TILE_ROWS:
            return cross_ref[22 + 3 * (i - TILE_ROWS) + part]
        if part == 1:
            return cross_ref[16 + min(max(i - skip, 0), 5)]
        return cross_ref[i + 4 * part]

    def received(e, part):
        at = slice(8 * part, 8 * part + 8)
        if e < -TILE_ROWS:
            i = e + TILE_ROWS + 2
            return [jnp.where(first_core, cross_ref[28 + m], far_ref[m]) for m in (i, 2, 3)]
        if e < 0:
            places = (e + TILE_ROWS, TILE_ROWS, TILE_ROWS + 1)
            return [jnp.where(first_core, cross_at(i, part, 2), partner_ref[i, at]) for i in places]
        if e < TILE_ROWS:
            return [own_ref[i, at, :] for i in (e, TILE_ROWS, TILE_ROWS + 1)]
        if e < 2 * TILE_ROWS:
            places = (e - TILE_ROWS, TILE_ROWS, TILE_ROWS + 1)
            return [jnp.where(first_core, partner_ref[i, at], cross_at(i, part, 0)) for i in places]
        i = e - 2 * TILE_ROWS
        return [jnp.where(first_core, far_ref[m], cross_ref[28 + m]) for m in (i, 2, 3)]

    for row in range(ALL_ROWS):
        e = row - FIRST
        near = e % TILE_ROWS
        for part in range(3 if -TILE_ROWS <= e < 2 * TILE_ROWS else 1):
            value, low, high = received(e, part)
            pair = (value, beside(low, high, near))
            for half in range(2):
                value = pair[half]
                if part == 0:
                    state_a[row, half] = value
                elif part == 1:
                    adjoint[row, half] = value
                else:
                    k0_ref[row, half] = jnp.broadcast_to(value[0:1], (8, LANES))
                    k1_ref[row, half] = jnp.broadcast_to(value[1:2], (8, LANES))
                    mask_ref[row, half] = jnp.where(
                        place, 1.0, jnp.where(speed, value[4:5], value[5:6])
                    )
                    sign_ref[row, half] = jnp.where((field == 2) | (field == 3), value, 0.0)

    def across(pair, step):
        turned = [roll(value, -step, 1) for value in pair]
        edge = lane >= LANES - step if step > 0 else lane < -step
        return jnp.where(edge, turned[1], turned[0]), jnp.where(edge, turned[0], turned[1])

    def both(ref, row):
        return ref[row, 0], ref[row, 1]

    def gather(total, value, entry):
        _, at, width = entry
        turned = roll(value, at + width, 1)
        return jnp.where((lane >= at) & (lane < at + 2 * width), turned, total)

    def scatter(value, entry):
        _, at, width = entry
        turned = roll(value, -(at + width), 1)
        return jnp.where((lane < width) | (lane >= LANES - width), turned, 0.0)

    def tile_lanes(tile):
        return slice(tile * LANES, (tile + 1) * LANES)

    gravity = jnp.where(field == 5, -GRAV, 0.0)
    keep = jnp.where(speed, DAMP, 1.0)

    def forward(k, state, target):
        plan = PLANS[k]
        x_ref = xs[k]
        moved = span((8, 6, 0)[k])
        packed = {tile: [zero, zero] for tile in plan.packed}
        for row in sorted(set(moved) | set(span(plan.reach))):
            here, up, down = both(state, row), both(state, row + 1), both(state, row - 1)
            right, left = across(here, 1), across(here, -1)
            update = row in moved
            if update:
                up2, down2 = both(state, row + 2), both(state, row - 2)
                right2, left2 = across(here, 2), across(here, -2)
            for half in range(2):
                s = here[half]
                twice = 2.0 * s
                lap_rows = up[half] + down[half] - twice
                lap_columns = right[half] + left[half] - twice
                slope_rows = 0.5 * (up[half] - down[half])
                slope_columns = 0.5 * (right[half] - left[half])
                if row in plan.tile:
                    mixed = jnp.where(field == 0, slope_rows, sign_ref[row, half])
                    mixed = jnp.where(field == 1, slope_columns, mixed)
                    mixed = jnp.where(field == 6, lap_rows, mixed)
                    mixed = jnp.where(field == 7, lap_columns, mixed)
                    if half == 0:
                        x_ref[:, tile_lanes(plan.tile[row])] = jnp.concatenate([s, mixed], axis=0).astype(BF16)
                    else:
                        for table in (plan.forward, plan.backward):
                            if row in table and (table is plan.forward or table[row] != plan.forward.get(row)):
                                entry = table[row]
                                old = packed[entry[0]]
                                packed[entry[0]] = [gather(old[0], s, entry), gather(old[1], mixed, entry)]
                if update and (half == 0 or k < 2):
                    bend = (up2[half] + down2[half] + right2[half] + left2[half]) - 4.0 * (
                        up[half] + down[half] + right[half] + left[half]
                    )
                    bend = bend + 12.0 * s
                    pull = k0_ref[row, half] * lap_rows + k1_ref[row, half] * lap_columns - KB * bend
                    turn = KC * jnp.where(field == 6, slope_rows, jnp.where(field == 7, slope_columns, 0.0))
                    force = roll(pull, 3, 0) + roll(turn, 5, 0) + gravity
                    rate = KS * jnp.where(field == 6, lap_rows, lap_columns)
                    change = jnp.where(speed, force, jnp.where(slide, rate, 0.0))
                    later[row, half] = keep * s + DT * change
        for tile, (top, bottom) in packed.items():
            x_ref[:, tile_lanes(tile)] = jnp.concatenate([top, bottom], axis=0).astype(BF16)

        def layer(z, keep_slope, block):
            bent = jnp.tanh(z)
            part = z * bent
            start, stop = block[0] * LANES, min(block[1], plan.saved) * LANES
            if stop > start:
                keep_slope[start:stop, :] = (1.0 + bent) * (1.0 + (z - part))
            return (z + part).astype(BF16)

        for block in plan.blocks:
            at = slice(block[0] * LANES, block[1] * LANES)
            act = layer(dot_columns(x_ref[:, at], w1_half), slopes_first[k], block)
            if block[0] == 0:
                act_first[k] = act
            act = layer(dot(act, w2), slopes_second[k], block)
            if block[0] == 0:
                act_second[k] = act
            if k < 2 or block[0] == 0:
                friction[:, at] = dot_rows(w3t, act)
        for row in moved:
            for half in range(2 if k < 2 else 1):
                value = later[row, half]
                if half == 0 and row in plan.tile:
                    value = value - DT * friction[:, tile_lanes(plan.tile[row])]
                if half == 1 and row in plan.forward:
                    entry = plan.forward[row]
                    value = value - DT * scatter(friction[:, tile_lanes(entry[0])], entry)
                value = mask_ref[row, half] * value
                value = value + jnp.where(place, DT * roll(value, 5, 0), 0.0)
                if k < 2:
                    target[row, half] = value
                else:
                    final_ref[0, :, row - FIRST, :] = value

    forward(0, state_a, state_b)
    forward(1, state_b, state_a)
    forward(2, state_a, None)
    final_copy = pltpu.make_async_copy(final_ref, final_hbm, sems.at[0])
    final_copy.start()

    def backward(k):
        plan = PLANS[k]
        inner, middle, outer = plan.back - 1, plan.back, plan.back + 1
        packed = zero
        for row in span(middle):
            for half in range(2):
                value = jnp.where(slide, -DT * adjoint[row, half], 0.0)
                if half == 0:
                    upstream[:, tile_lanes(plan.tile[row])] = jnp.concatenate([value, zero], axis=0).astype(BF16)
                elif row in plan.backward:
                    packed = gather(packed, value, plan.backward[row])
        upstream[:, tile_lanes(plan.near)] = jnp.concatenate([packed, zero], axis=0).astype(BF16)
        for start, stop in ((0, TILE_ROWS), (TILE_ROWS, plan.near + 1)):
            at = slice(start * LANES, stop * LANES)
            second_back = (dot_columns(upstream[:, at], w3) * slopes_second[k][at, :]).astype(BF16)
            first_back = (dot_rows(second_back, w2) * slopes_first[k][at, :]).astype(BF16)
            feature_back[:, at] = dot_rows(w1, first_back)
            if start == 0:
                second = dot_columns(act_first[k], second_back)
                first = dot(xs[k][:, at], first_back)
                third = dot(upstream[:, at], act_second[k])
        if k == 2:
            total_second[...], total_first[...], total_third[...] = second, first, third
        else:
            total_second[...] += second
            total_first[...] += first
            total_third[...] += third

        for row in span(outer):
            for half in range(2):
                q = adjoint[row, half]
                total = mask_ref[row, half] * (q + DT * roll(q, 3, 0))
                force_ref[row, half] = jnp.where(place, DT * roll(total, 5, 0), 0.0)
                if distance(row) <= inner:
                    sum_ref[row, half] = jnp.where(speed, DAMP * total, q)
        for row in span(middle):
            force = both(force_ref, row)
            high, low = [], []
            for half in range(2):
                q, g = adjoint[row, half], force[half]
                if half == 0:
                    at = tile_lanes(plan.tile[row])
                    straight, mixed = feature_back[0:8, at], feature_back[8:16, at]
                elif row in plan.backward:
                    entry = plan.backward[row]
                    at = tile_lanes(entry[0])
                    straight, mixed = scatter(feature_back[0:8, at], entry), scatter(feature_back[8:16, at], entry)
                else:
                    straight, mixed = zero, zero
                carried = DT * KS * q + mixed
                by_rows = k0_ref[row, half] * g + jnp.where(field == 6, carried, 0.0)
                by_columns = k1_ref[row, half] * g + jnp.where(field == 7, carried, 0.0)
                tilt = 0.5 * jnp.where(slide, KC * roll(g, 6, 0), mixed)
                tilt_rows = jnp.where((field == 0) | (field == 6), tilt, 0.0)
                tilt_columns = jnp.where((field == 1) | (field == 7), tilt, 0.0)
                ahead_ref[row, half] = by_rows + 4.0 * KB * g - tilt_rows
                behind_ref[row, half] = by_rows + 4.0 * KB * g + tilt_rows
                high.append(by_columns + 4.0 * KB * g - tilt_columns)
                low.append(by_columns + 4.0 * KB * g + tilt_columns)
                if distance(row) <= inner:
                    center = -2.0 * (by_rows + by_columns) - 12.0 * KB * g
                    sum_ref[row, half] = sum_ref[row, half] + straight + center
            if distance(row) <= inner:
                right, left = across(high, 1), across(low, -1)
                right2, left2 = across(force, 2), across(force, -2)
                for half in range(2):
                    sideways = right[half] + left[half] - KB * (right2[half] + left2[half])
                    sum_ref[row, half] = sum_ref[row, half] + sideways
        for row in span(inner):
            for half in range(2 if k > 0 else 1):
                value = sum_ref[row, half] + ahead_ref[row + 1, half] + behind_ref[row - 1, half]
                value = value - KB * (force_ref[row + 2, half] + force_ref[row - 2, half])
                if k > 0:
                    adjoint[row, half] = jnp.where(slide, mask_ref[row, half] * value, value)
                else:
                    adjoint_ref[0, :, row - FIRST, :] = value

    backward(2)
    backward(1)
    backward(0)
    adjoint_copy = pltpu.make_async_copy(adjoint_ref, adjoint_hbm, sems.at[1])
    adjoint_copy.start()

    small = total_first[...]
    third = total_third[0:8, :]
    row_index = lax.broadcasted_iota(jnp.int32, (8, HID), 0)
    top = jnp.where(row_index < 2, pltpu.roll(third, 2, 0), small[0:8])
    bottom = small[8:16]
    for c in range(HID // 8):
        for j in range(8):
            at = 8 * c + (2 * j) % 8
            side = slice(0, LANES) if j < 4 else slice(LANES, HID)
            grads_ref[c, j] = total_second[at : at + 2, side]
        line = (top if c < 16 else bottom)[(c // 2) % 8 : (c // 2) % 8 + 1, (c % 2) * LANES : (c % 2 + 1) * LANES]
        grads_ref[c, 8] = jnp.broadcast_to(line, (2, LANES))
    final_copy.wait()
    adjoint_copy.wait()


def run_main(*operands):
    rows = (ALL_ROWS, 2, 8, LANES)
    scratch = [pltpu.VMEM((1, 8, TILE_ROWS, LANES), F32)] * 2 + [pltpu.SemaphoreType.DMA((2,))]
    scratch += [pltpu.VMEM(rows, F32) for _ in range(12)]
    scratch += [pltpu.VMEM((16, plan.tiles * LANES), BF16) for plan in PLANS]
    scratch += [pltpu.VMEM((plan.saved * LANES, HID), F32) for plan in PLANS] * 2
    scratch += [pltpu.VMEM((3, OWN, HID), BF16)] * 2
    scratch += [
        pltpu.VMEM((8, PLANS[0].tiles * LANES), F32),
        pltpu.VMEM((16, PLANS[2].tiles * LANES), BF16),
        pltpu.VMEM((16, PLANS[2].tiles * LANES), F32),
        pltpu.VMEM((HID, HID), F32),
        pltpu.VMEM((16, HID), F32),
        pltpu.VMEM((16, HID), F32),
    ]
    return pl.pallas_call(
        main_kernel,
        out_shape=(
            jax.ShapeDtypeStruct((1, 8, TILE_ROWS, LANES), F32),
            jax.ShapeDtypeStruct((1, 8, TILE_ROWS, LANES), F32),
            jax.ShapeDtypeStruct((HID // 8, 9, 2, LANES), F32),
        ),
        in_specs=[pl.BlockSpec(memory_space=pltpu.SMEM if i == 1 else pltpu.VMEM) for i in range(len(operands))],
        out_specs=[pl.BlockSpec(memory_space=m) for m in (pltpu.HBM, pltpu.HBM, pltpu.VMEM)],
        scratch_shapes=scratch,
        compiler_params=pltpu.CompilerParams(vmem_limit_bytes=40 << 20),
        name="substeps",
    )(*operands)


def run_pack(*operands):
    return pl.pallas_call(
        pack_kernel,
        out_shape=(
            jax.ShapeDtypeStruct((TILE_ROWS, 24, LANES), F32),
            jax.ShapeDtypeStruct((24, LANES), F32),
            jax.ShapeDtypeStruct((24, LANES), F32),
            jax.ShapeDtypeStruct((1, 24, LANES), F32),
        ),
        in_specs=[pl.BlockSpec(memory_space=pltpu.HBM)] * 6,
        scratch_shapes=[pltpu.VMEM(value.shape, value.dtype) for value in operands]
        + [pltpu.SemaphoreType.DMA((6,))],
        compiler_params=pltpu.CompilerParams(vmem_limit_bytes=4 << 20),
        name="pack_tile",
    )(*[pltpu.with_memory_space_constraint(value, pltpu.HBM) for value in operands])


def shift(value, axis, step):
    count = lax.axis_size(axis)
    return lax.ppermute(value, axis, [(i, i + step) for i in range(count) if 0 <= i + step < count])


def sum_everywhere(part):
    plane, column = lax.axis_size(PLANE), lax.axis_size(COLUMN)
    part = jnp.sum(lax.all_to_all(part, PLANE, 0, 0, tiled=True), axis=0)
    part = jnp.broadcast_to(part, (column,) + part.shape)
    part = jnp.sum(lax.all_to_all(part, COLUMN, 0, 0, tiled=True), axis=0)
    part = jnp.broadcast_to(part, (plane,) + part.shape)
    return lax.all_to_all(part, PLANE, 0, 0, tiled=True)


def finish_kernel(scale, flat_ref, first_ref, second_ref, third_ref):
    for c in range(HID // 8):
        for j in range(8):
            at = 8 * c + (2 * j) % 8
            side = slice(0, LANES) if j < 4 else slice(LANES, HID)
            second_ref[at : at + 2, side] = flat_ref[c, j] * scale
    for half in range(2):
        at = slice(half * LANES, (half + 1) * LANES)
        for f, row in enumerate(FEATURE_ROWS):
            first_ref[f : f + 1, at] = flat_ref[2 * row + half, 8, 0:1, :] * scale
        for f in range(2):
            third_ref[f : f + 1, at] = flat_ref[2 * f + half, 8, 0:1, :] * scale


def shards(state, adjoint, stiffness, pinned, weave, first_weight, second_weight, third_weight):
    own, low_edge, high_edge, last = run_pack(state, adjoint, stiffness, pinned, weave, third_weight.T)
    left = shift(high_edge, WEFT, 1)
    right = shift(low_edge, WEFT, -1)
    own = jnp.concatenate([own, left[None], right[None], last], axis=0)
    count = lax.axis_size(WARP)
    core = lax.axis_index(WARP) % 2
    mates = [(i, i ^ 1) for i in range(count)]
    partner = lax.ppermute(own, WARP, mates)
    outward = lax.dynamic_slice_in_dim(partner, core * (TILE_ROWS - 2), 2, axis=0)[:, 0:8]
    parts = own[:TILE_ROWS].reshape(TILE_ROWS, 3, 8, LANES)
    near = lax.dynamic_slice_in_dim(parts[:, 1], core * 2, 6, axis=0)
    sides = [left.reshape(3, 8, LANES), right.reshape(3, 8, LANES)]
    wide = jnp.concatenate(
        [parts[:, 0], parts[:, 2], near, *sides, outward, partner[TILE_ROWS : TILE_ROWS + 2, 0:8]], axis=0
    )
    pairs = [(i, j) for i in range(count) for j in [((i + 1) ^ 1) - 1] if 0 <= j < count]
    cross = lax.ppermute(wide, WARP, pairs)
    inward = lax.dynamic_slice_in_dim(cross, (1 - core) * (TILE_ROWS - 2), 2, axis=0)
    far = lax.ppermute(jnp.concatenate([inward, cross[22:23], cross[25:26]], axis=0), WARP, mates)

    final_state, state_adjoint, grads = run_main(
        own, core.reshape(1), partner, cross, far, first_weight, second_weight
    )
    flat = sum_everywhere(grads)
    cells = OWN * lax.axis_size(WARP) * lax.axis_size(WEFT)
    first, second, third = pl.pallas_call(
        functools.partial(finish_kernel, float(cells) ** -0.5),
        out_shape=(
            jax.ShapeDtypeStruct((12, HID), F32),
            jax.ShapeDtypeStruct((HID, HID), F32),
            jax.ShapeDtypeStruct((2, HID), F32),
        ),
        compiler_params=pltpu.CompilerParams(vmem_limit_bytes=4 << 20),
        name="unpack_grads",
    )(flat)
    return final_state, state_adjoint, first, second, third.T


def factors(mesh):
    warp, weft = mesh.shape["warp"], mesh.shape["weft"]
    zlo = 4 if weft % 4 == 0 else 1
    x = 4 if warp % 8 == 0 else 1
    core = 2 if warp % 2 == 0 else 1
    return (warp // (x * core), x, core, weft // zlo, zlo)


def solution(mesh):
    fine = Mesh(mesh.devices.reshape(factors(mesh)), WARP + WEFT)
    field = P(None, None, WARP, WEFT)
    placed = (field, field, P(None, WARP, WEFT), P(None, WARP, WEFT), P(WARP, WEFT), P(), P(), P())
    return jax.shard_map(
        shards,
        mesh=fine,
        in_specs=placed,
        out_specs=(field, field, P(), P(), P()),
        check_vma=False,
    )
```
